32 devices in a mesh: groups: 2 (over x), wide: 16 (over z, y, core).
Axes of the slice: x: 2, y: 2, z: 4, core: 2. Of those that a mesh axis runs over, the one named last changes fastest.
Arguments:
- hidden_states: bfloat16 [2048, 64, 1024], P(('groups', 'wide')), parts along dimension 0, may hold values from -6 to 6
- block_owner: int32 [2048, 1], P(('groups', 'wide')), parts along dimension 0, may hold values from 0 to 15; in each aligned block of 64 rows (0 to 63, 64 to 127, ...) at most 8 rows name the same one
- token_doc: int32 [2048, 64], P(('groups', 'wide')), parts along dimension 0, may hold values from 0 to 7, never falling along the last dimension, each value on 1 to 32 neighbouring positions
- token_live: int32 [2048, 64], P(('groups', 'wide')), parts along dimension 0, may hold values 0 or 1
- proj_weight: bfloat16 [1024, 128], replicated, may hold values from -0.1875 to 0.1875
- queries: bfloat16 [2048, 128], P(('groups', 'wide')), parts along dimension 0, may hold values from -1.5 to 1.5
Outputs:
- scores: float32 [256, 1024], P(('groups', 'wide')), parts along dimension 0
The draws below stay inside these ranges and needn't reach their ends.
There are 2 independent parts, one for each index of `groups`. The reference program is written for one: setup_inputs(seed, part) draws one part's arguments, and reference() takes and returns one part's arrays. A program takes and returns all parts, laid end to end along the dimension named above; an argument that names none is the same for every part. Nothing has to cross between parts.
Inputs may be any that keep to these rules, and one draw needn't show every extreme that they name: `block_owner`: among the 64 blocks of one index of wide no owner is named by more than 8 blocks, a bound that some block reaches. `token_doc`: within a block the ids never fall and every id appears.
All inputs are finite; a program needn't handle non-finite values. No bound on the sum of `token_live` on one device may be relied on, other than what follows from the above.
Results may differ from the reference program's by a relative error of at most 0.0011.
Values may be sent and summed in bfloat16 or wider, within the bound.
No kernel may reach another device: no remote copies, remote signals or barrier semaphores. Data moves between devices by JAX's collectives and lax.ppermute only.
A program may use at most 64 MiB of HBM per device.

```python
import math
import jax
import jax.numpy as jnp
import numpy as np
from jax import lax

D = 1024
DIM = 128
BLOCK = 64
B_DEV = 64
DOC_DEV = 8
MOST = 8
BLOCKS = 1024
QUERIES = 1024
DOCS = 128
N_WIDE = 16


def place_ends(entries, stream_key, low, top_value):
    place = [jax.random.randint(jax.random.fold_in(stream_key, axis), (), 0, length) for axis, length in enumerate(entries.shape)]
    widest = entries.shape.index(max(entries.shape))
    next_to = place[:widest] + [(place[widest] + 1) % entries.shape[widest]] + place[widest + 1:]
    return entries.at[tuple(place)].set(low).at[tuple(next_to)].set(top_value)


def levels(own_key, extent, shards, low, top_value):
    factor_of, own = 1.0, jax.random.fold_in(own_key, 6)
    for dim, shards_of in shards:
        steps = jnp.exp(jax.random.uniform(jax.random.fold_in(own, dim), (shards_of,), jnp.float32, low / len(shards), top_value / len(shards)))
        factor_of = factor_of * jnp.repeat(steps, extent[dim] // shards_of).reshape([-1 if axis == dim else 1 for axis in range(len(extent))])
    return factor_of


def length_profile(number_of, total, most, skew):
    portions = [(1 << 20) // math.isqrt(rank ** skew) + 1 for rank in range(2, number_of + 1)]
    spare, counts = total - most - (number_of - 1), [1] * (number_of - 1)
    while spare > 0:
        movable = [i for i in range(number_of - 1) if counts[i] < most]
        mass, budget = sum([portions[i] for i in movable]), spare
        for i in movable:
            addition = min(most - counts[i], max(1, budget * portions[i] // mass), spare)
            counts[i] = counts[i] + addition
            spare = spare - addition
    return np.array([most] + counts)


def uneven_parts(rng, amount, total, limit, skew):
    if amount == 2:
        one = jax.random.randint(rng, (), max(1, total - limit), min(limit, total - 1) + 1)
        return jnp.stack([one, total - one])
    sizes = jnp.asarray(length_profile(amount, total, limit, skew), jnp.int32)
    pairs = (amount - 1) // 2
    donor, taker = sizes[1:1 + 2 * pairs:2], sizes[2:2 + 2 * pairs:2]
    margin = jnp.minimum(donor - 1, limit - taker)
    shifted = jax.random.randint(jax.random.fold_in(rng, 1), (pairs,), 0, 1 << 20) % (margin + 1)
    sizes = sizes.at[1:1 + 2 * pairs:2].set(donor - shifted).at[2:2 + 2 * pairs:2].set(taker + shifted)
    return sizes[jax.random.permutation(jax.random.fold_in(rng, 2), amount)]


def deal_out(stream_key, own, number, rows, amount, top, limit, skew):
    sequence = jax.random.permutation(stream_key, amount)
    packed, ordinary = shares(amount, rows * top, limit, skew, True), shares(amount, rows * top, limit, skew, False)
    places = jnp.arange(amount)

    def named(sizes, turn):
        used = int((sizes > 0).sum())
        fixed = max(1, used // 4)
        shifted = fixed + (places - fixed + turn * (used - fixed)) % max(1, amount - fixed)
        return jnp.zeros((amount,), jnp.int32).at[sequence[jnp.where(places < fixed, places, shifted)]].set(jnp.asarray(sizes, jnp.int32))

    sizes = jnp.where(number % 4 == 0, named(packed, number // 4), named(ordinary, number - number // 4 - 1))
    mixed = jax.random.permutation(jax.random.fold_in(own, 3), amount)
    source_of, receiver = mixed[0:amount // 2 * 2:2], mixed[1:amount // 2 * 2:2]
    margin = jnp.minimum(sizes[source_of] - 1, limit - sizes[receiver]) // 2
    margin = jnp.where((source_of == sequence[0]) | (receiver == sequence[0]) | (sizes[receiver] == 0), 0, jnp.maximum(margin, 0))
    shifted = jax.random.randint(jax.random.fold_in(own, 4), (amount // 2,), 0, 1 << 20) % (margin + 1)
    sizes = sizes.at[source_of].add(-shifted).at[receiver].add(shifted)
    items = jnp.searchsorted(jnp.cumsum(sizes), jnp.arange(rows * top), side="right").astype(jnp.int32)
    listing = items.reshape(top, rows).T
    listing = listing[jax.random.permutation(jax.random.fold_in(own, 1), rows)]
    turn = jax.random.randint(jax.random.fold_in(own, 2), (rows, 1), 0, top)
    return jnp.take_along_axis(listing, (jnp.arange(top)[None, :] + turn) % top, axis=1)


def shares(number_of, total, bound, skew, full):
    loads = [(1 << 20) // math.isqrt(grade ** skew) + 1 for grade in range(1, number_of + 1)]
    largest = bound if full else min(bound, max(-(-total // number_of), total * loads[0] // sum(loads)))
    least = 1 if total - largest >= number_of - 1 else 0
    given, surplus = [largest] + [least] * (number_of - 1), total - largest - least * (number_of - 1)
    while surplus > 0:
        candidates = [i for i in range(1, number_of) if given[i] < largest] or [i for i in range(1, number_of) if given[i] < bound]
        whole, budget = sum([loads[i] for i in candidates]), surplus
        for i in candidates:
            addition = min(bound - given[i], max(1, budget * loads[i] // whole), surplus)
            given[i] = given[i] + addition
            surplus = surplus - addition
    return np.array(given)


def scatter_about(own_key, dims, spread, most, pieces=(), dtype=jnp.bfloat16):
    result = spread * jax.random.normal(own_key, dims, jnp.float32)
    if pieces:
        result = result * levels(own_key, dims, pieces, -0.22, 0.18)
    return jnp.clip(result, -most, most).astype(dtype)


def setup_inputs(seed: int = 0, part: int = 0) -> dict:
    streams_of = jax.random.split(jax.random.key(seed), 7)
    part_keys = jax.random.split(jax.random.fold_in(streams_of[6], part), 7)
    hidden_states = scatter_about(part_keys[0], (BLOCKS, BLOCK, D), 1.0, 6.0, ((0, 16),))
    block_owner_keys = jax.random.split(jax.random.fold_in(part_keys[1], 1), BLOCKS // B_DEV)
    block_owner_turns = jax.random.permutation(jax.random.fold_in(part_keys[1], 3), BLOCKS // B_DEV)
    block_owner = jax.vmap(lambda own, number: deal_out(jax.random.fold_in(part_keys[1], 2), own, number, B_DEV, N_WIDE, 1, MOST, 2))(block_owner_keys, block_owner_turns).reshape((BLOCKS, 1))
    token_doc = jax.vmap(lambda own: jnp.searchsorted(jnp.cumsum(uneven_parts(own, DOC_DEV, BLOCK, BLOCK // 2, 2)), jnp.arange(BLOCK), side="right"))(jax.random.split(part_keys[2], BLOCKS)).reshape((BLOCKS, BLOCK)).astype(jnp.int32)
    token_live = place_ends((jax.random.randint(part_keys[3], (BLOCKS, BLOCK), 0, 8) < 7).astype(jnp.int32), jax.random.fold_in(part_keys[3], 1), 0, 1)
    proj_weight = scatter_about(streams_of[4], (D, DIM), D ** -0.5, 0.1875)
    queries = scatter_about(part_keys[5], (QUERIES, DIM), 0.25, 1.5, ((0, 16),))
    return {"hidden_states": hidden_states, "block_owner": block_owner, "token_doc": token_doc, "token_live": token_live, "proj_weight": proj_weight, "queries": queries}


def reference(hidden_states, block_owner, token_doc, token_live, proj_weight, queries):
    nblocks, block_len, model_width = hidden_states.shape
    projected = jnp.dot(hidden_states.reshape(nblocks * block_len, model_width), proj_weight, preferred_element_type=jnp.float32)
    vectors = projected * lax.rsqrt(lax.optimization_barrier(jnp.sum(projected * projected, axis=1, keepdims=True)) + 1e-06)
    vectors = vectors.astype(jnp.bfloat16).reshape(nblocks, block_len, -1)
    doc_code = jnp.where(token_live == 1, token_doc, -1).astype(jnp.int32)
    owners = block_owner[:, 0].astype(jnp.int32)
    query_count = queries.shape[0]

    def visit(table, group_item):
        block_vec, block_code, owner = group_item
        similar = lax.dot_general(queries.astype(jnp.float32), block_vec.astype(jnp.float32), (((1,), (1,)), ((), ())))
        partial_value = jnp.stack([lax.optimization_barrier(jnp.max(jnp.where(block_code[None, :] == doc_slot, similar, -1000000000.0), axis=1)) for doc_slot in range(DOC_DEV)])
        first_row = (owner * DOC_DEV).astype(jnp.int32)
        current = lax.dynamic_slice(table, (first_row, jnp.int32(0)), (DOC_DEV, query_count))
        table = lax.dynamic_update_slice(table, jnp.maximum(current, partial_value), (first_row, jnp.int32(0)))
        return (table, None)
    start_table = jnp.full((DOCS, query_count), -1000000000.0, jnp.float32)
    table, unused = lax.scan(visit, start_table, (vectors, doc_code, owners))
    return jnp.where(table > -100000000.0, table, jnp.float32(0.0))
```

```python
import functools

import jax
import jax.numpy as jnp
from jax import lax
from jax.experimental import pallas as pl
from jax.experimental.pallas import tpu as pltpu
from jax.sharding import PartitionSpec as P

DOC_DEV = 8
CHUNK = 8
LOW = -1000000000.0


def bit_reverse(value, bits):
    out = value * 0
    for bit in range(bits):
        out = out | (((value >> bit) & 1) << (bits - 1 - bit))
    return out


def pack_kernel(h_ref, w_ref, doc_ref, live_ref, out_ref, meta_ref):
    nb, bl, d = h_ref.shape
    dim = w_ref.shape[1]
    projected = jnp.dot(
        h_ref[...].reshape(nb * bl, d), w_ref[...], preferred_element_type=jnp.float32
    )
    total = jnp.sum(projected * projected, axis=1, keepdims=True)
    vectors = (projected * lax.rsqrt(total + 1e-06)).astype(jnp.bfloat16)
    doc = doc_ref[...]
    live = live_ref[...] == 1
    livef = live.astype(jnp.float32)
    upto = lax.broadcasted_iota(jnp.int32, (bl, bl), 0) <= lax.broadcasted_iota(
        jnp.int32, (bl, bl), 1
    )
    counted = jnp.dot(livef, upto.astype(jnp.float32), preferred_element_type=jnp.float32)
    before = jnp.zeros((nb, bl), jnp.float32)
    extra = jnp.zeros((nb, bl), jnp.int32)
    for slot in range(DOC_DEV):
        n = jnp.sum(jnp.where(doc == slot, livef, 0.0), axis=1, keepdims=True)
        more = jnp.maximum((n.astype(jnp.int32) - 1) >> 3, 0)
        before = before + jnp.where(doc > slot, n, 0.0)
        extra = extra + jnp.where(doc > slot, more, 0)
    rank = (counted - livef - before).astype(jnp.int32)
    part, group = rank >> 3, rank & 7
    row = jnp.where(part == 0, group * 8 + doc, 64 + group * 8 + extra + part - 1)
    row = jnp.where(live, row, -1)
    live_doc = jnp.where(live, doc, -1)
    sub = lax.broadcasted_iota(jnp.int32, (8, bl), 0)
    earlier = (
        lax.broadcasted_iota(jnp.int32, (8, 8), 0) > lax.broadcasted_iota(jnp.int32, (8, 8), 1)
    ).astype(jnp.float32)
    for b in range(nb):
        tiles, counts = [], []
        for tile in range(2):
            hits = [
                (row[b : b + 1] == sub + (64 * tile + 8 * g)).astype(jnp.float32)
                for g in range(CHUNK)
            ]
            count = jnp.sum(functools.reduce(jnp.add, hits), axis=1, keepdims=True)
            counts.append(count)
            tiles += hits[:1]
            tiles += [jnp.where(count > float(g), hits[g], hits[0]) for g in range(1, CHUNK)]
        pick = jnp.concatenate(tiles, axis=0).astype(jnp.bfloat16)
        out_ref[b] = jnp.dot(
            pick, vectors[b * bl : (b + 1) * bl], preferred_element_type=jnp.float32
        ).astype(jnp.bfloat16)
        n = jnp.sum((live_doc[b : b + 1] == sub).astype(jnp.float32), axis=1, keepdims=True)
        n = jnp.broadcast_to(n, (8, dim)).astype(jnp.int32)
        more = jnp.maximum((n - 1) >> 3, 0)
        first = jnp.dot(
            earlier, more.astype(jnp.float32), preferred_element_type=jnp.float32
        ).astype(jnp.int32)
        for tile in range(2):
            meta_ref[b, tile] = jnp.broadcast_to((counts[tile] > 0).astype(jnp.int32), (8, dim))
        for j in range(3):
            meta_ref[b, 2 + j] = jnp.where(more > j, first + j, 7)


def pack(hidden_states, proj_weight, token_doc, token_live):
    nb, bl, d = hidden_states.shape
    dim = proj_weight.shape[1]
    step = 16
    return pl.pallas_call(
        pack_kernel,
        grid=(nb // step,),
        in_specs=[
            pl.BlockSpec((step, bl, d), lambda i: (i, 0, 0)),
            pl.BlockSpec((d, dim), lambda i: (0, 0)),
            pl.BlockSpec((step, bl), lambda i: (i, 0)),
            pl.BlockSpec((step, bl), lambda i: (i, 0)),
        ],
        out_specs=[
            pl.BlockSpec((step, 128, dim), lambda i: (i, 0, 0)),
            pl.BlockSpec((step, 5, 8, dim), lambda i: (i, 0, 0, 0)),
        ],
        out_shape=[
            jax.ShapeDtypeStruct((nb, 128, dim), jnp.bfloat16),
            jax.ShapeDtypeStruct((nb, 5, 8, dim), jnp.int32),
        ],
        cost_estimate=pl.CostEstimate(
            flops=2 * nb * bl * d * dim, bytes_accessed=2 * nb * bl * d, transcendentals=nb * bl
        ),
        name="pack",
    )(hidden_states, proj_weight, token_doc, token_live)


def score_kernel(
    owner_ref, vec_ref, meta_ref, got_ref, keep_ref, send_ref, query_ref, table_ref, *, width
):
    n = lax.axis_size("wide")
    bits = n.bit_length() - 1
    me = lax.axis_index("wide")
    nb = vec_ref.shape[0]
    columns = got_ref.shape[0]
    piece = columns // n
    for j in range(n):
        device = me ^ bit_reverse(j, bits)
        query_ref[pl.ds(pl.multiple_of(device * piece, piece), piece), :] = got_ref[
            j * piece : (j + 1) * piece, :
        ]
    table_ref[...] = jnp.full(table_ref.shape, LOW, jnp.float32)
    span = min(columns, 1024)

    def visit(b, start):
        place = bit_reverse(owner_ref[b] ^ me, bits)
        rows = pl.ds(pl.multiple_of(place * DOC_DEV, DOC_DEV), DOC_DEV)
        some = [meta_ref[b, tile] > 0 for tile in range(2)]
        index = [meta_ref[b, 2 + j] for j in range(3)]
        tokens = vec_ref[b]
        for t in range(span // width):
            at = pl.ds(start + t * width, width)
            similar = lax.dot_general(
                tokens,
                query_ref[at, :],
                (((1,), (1,)), ((), ())),
                preferred_element_type=jnp.float32,
            )
            first, rest = (
                functools.reduce(
                    jnp.maximum,
                    [similar[64 * tile + 8 * g : 64 * tile + 8 * g + 8] for g in range(CHUNK)],
                )
                for tile in range(2)
            )
            best = []
            for c in range(width // 128):
                top = jnp.where(some[0], first[:, c * 128 : (c + 1) * 128], LOW)
                further = jnp.where(some[1], rest[:, c * 128 : (c + 1) * 128], LOW)
                for j in range(3):
                    top = jnp.maximum(top, jnp.take_along_axis(further, index[j], axis=0))
                best.append(top)
            table_ref[rows, at] = jnp.maximum(table_ref[rows, at], jnp.concatenate(best, axis=1))

    def over_blocks(start):
        def some_blocks(i, carry):
            for u in range(8):
                visit(i * 8 + u, start)
            return carry

        lax.fori_loop(0, nb // 8, some_blocks, 0)

    if columns == span:
        over_blocks(0)
    else:

        def one_span(i, carry):
            over_blocks(pl.multiple_of(i * span, span))
            return carry

        lax.fori_loop(0, columns // span, one_span, 0)
    half = table_ref.shape[0] // 2
    keep_ref[...] = table_ref[:half, :]
    send_ref[...] = table_ref[half:, :]


def score(owner, packed, meta, gathered, owners):
    nb, rows, dim = packed.shape
    columns = gathered.shape[0]
    half = jax.ShapeDtypeStruct((owners * DOC_DEV // 2, columns), jnp.float32)
    vmem = pl.BlockSpec(memory_space=pltpu.VMEM)
    return pl.pallas_call(
        functools.partial(score_kernel, width=256),
        in_specs=[pl.BlockSpec(memory_space=pltpu.SMEM), vmem, vmem, vmem],
        out_specs=[vmem, vmem],
        out_shape=[half, half],
        scratch_shapes=[
            pltpu.VMEM((columns, dim), jnp.bfloat16),
            pltpu.VMEM((owners * DOC_DEV, columns), jnp.float32),
        ],
        cost_estimate=pl.CostEstimate(
            flops=2 * nb * rows * dim * columns,
            bytes_accessed=2 * nb * rows * dim,
            transcendentals=0,
        ),
        name="score",
    )(owner, packed, meta, gathered)


def local(hidden_states, block_owner, token_doc, token_live, proj_weight, queries):
    n = lax.axis_size("wide")
    if n & (n - 1):
        raise ValueError("wide size")

    def swap(x, stride):
        return lax.ppermute(x, "wide", [(i, i ^ stride) for i in range(n)])

    strides = [1 << bit for bit in range(n.bit_length() - 1)]
    gathered = queries
    for stride in reversed(strides):
        gathered = jnp.concatenate([gathered, swap(gathered, stride)], axis=0)
    packed, meta = pack(hidden_states, proj_weight, token_doc, token_live)
    keep, send = score(block_owner.reshape(-1), packed, meta, gathered, n)
    for stride in strides:
        best = jnp.maximum(keep, swap(send, stride))
        half = best.shape[0] // 2
        if stride != strides[-1]:
            keep, send = best[:half], best[half:]
    return jnp.where(best > -100000000.0, best, jnp.float32(0.0))


def solution(mesh):
    placed = (
        P(("groups", "wide"), None, None),
        P(("groups", "wide"), None),
        P(("groups", "wide"), None),
        P(("groups", "wide"), None),
        P(),
        P(("groups", "wide"), None),
    )
    return jax.shard_map(
        local, mesh=mesh, in_specs=placed, out_specs=P(("groups", "wide"), None), check_vma=False
    )
```

```python
import functools

import jax
import jax.numpy as jnp
from jax import lax
from jax.experimental import pallas as pl
from jax.experimental.pallas import tpu as pltpu
from jax.sharding import PartitionSpec as P


DOC_DEV = 8
CHUNK = 8
GROUP = 8
UNROLL = 16
LOW = -1000000000.0
PARTS = (3, 3, 2)

VMEM = pl.BlockSpec(memory_space=pltpu.VMEM)
PARAMS = pltpu.CompilerParams(vmem_limit_bytes=24 << 20)


def bit_reverse(value, bits):
    out = value * 0
    for bit in range(bits):
        out = out | (((value >> bit) & 1) << (bits - 1 - bit))
    return out


def pack_kernel(
    h_hbm, w_hbm, doc_hbm, live_hbm, out_ref, meta_ref, h_ref, w_ref, doc_ref, live_ref, sems, *, start
):
    nb, bl, d = h_ref.shape
    dim = w_ref.shape[1]
    small = [
        pltpu.make_async_copy(w_hbm, w_ref, sems.at[0]),
        pltpu.make_async_copy(doc_hbm.at[pl.ds(start, nb)], doc_ref, sems.at[1]),
        pltpu.make_async_copy(live_hbm.at[pl.ds(start, nb)], live_ref, sems.at[2]),
    ]
    large = [
        pltpu.make_async_copy(
            h_hbm.at[pl.ds(start + g * GROUP, GROUP)], h_ref.at[pl.ds(g * GROUP, GROUP)], sems.at[3 + g]
        )
        for g in range(nb // GROUP)
    ]
    for copy in small + large:
        copy.start()
    for copy in small[1:]:
        copy.wait()
    sub = lax.broadcasted_iota(jnp.int32, (8, bl), 0)
    earlier = (
        lax.broadcasted_iota(jnp.int32, (8, 8), 0) > lax.broadcasted_iota(jnp.int32, (8, 8), 1)
    ).astype(jnp.float32)
    doc = doc_ref[...]
    live = live_ref[...] == 1
    livef = live.astype(jnp.float32)
    upto = lax.broadcasted_iota(jnp.int32, (bl, bl), 0) <= lax.broadcasted_iota(
        jnp.int32, (bl, bl), 1
    )
    counted = jnp.dot(livef, upto.astype(jnp.float32), preferred_element_type=jnp.float32)
    before = jnp.zeros((nb, bl), jnp.float32)
    extra = jnp.zeros((nb, bl), jnp.int32)
    for slot in range(DOC_DEV):
        n = jnp.sum(jnp.where(doc == slot, livef, 0.0), axis=1, keepdims=True)
        more = jnp.maximum((n.astype(jnp.int32) - 1) >> 3, 0)
        before = before + jnp.where(doc > slot, n, 0.0)
        extra = extra + jnp.where(doc > slot, more, 0)
    rank = (counted - livef - before).astype(jnp.int32)
    part, group = rank >> 3, rank & 7
    row = jnp.where(part == 0, group * 8 + doc, 64 + group * 8 + extra + part - 1)
    row = jnp.where(live, row, -1)
    live_doc = jnp.where(live, doc, -1)
    small[0].wait()
    for g in range(nb // GROUP):
        large[g].wait()
        projected = jnp.dot(
            h_ref[g * GROUP : (g + 1) * GROUP].reshape(GROUP * bl, d),
            w_ref[...],
            preferred_element_type=jnp.float32,
        )
        total = jnp.sum(projected * projected, axis=1, keepdims=True)
        vectors = (projected * lax.rsqrt(total + 1e-06)).astype(jnp.bfloat16)
        for u in range(GROUP):
            b = g * GROUP + u
            tiles, counts = [], []
            for tile in range(2):
                hits = [
                    (row[b : b + 1] == sub + (64 * tile + 8 * g8)).astype(jnp.float32)
                    for g8 in range(CHUNK)
                ]
                count = jnp.sum(functools.reduce(jnp.add, hits), axis=1, keepdims=True)
                counts.append(count)
                tiles += hits[:1]
                tiles += [jnp.where(count > float(i), hits[i], hits[0]) for i in range(1, CHUNK)]
            pick = jnp.concatenate(tiles, axis=0).astype(jnp.bfloat16)
            out_ref[b] = jnp.dot(
                pick, vectors[u * bl : (u + 1) * bl], preferred_element_type=jnp.float32
            ).astype(jnp.bfloat16)
            n = jnp.sum((live_doc[b : b + 1] == sub).astype(jnp.float32), axis=1, keepdims=True)
            n = jnp.broadcast_to(n, (8, dim)).astype(jnp.int32)
            more = jnp.maximum((n - 1) >> 3, 0)
            first = jnp.dot(
                earlier, more.astype(jnp.float32), preferred_element_type=jnp.float32
            ).astype(jnp.int32)
            for tile in range(2):
                meta_ref[b, tile] = jnp.broadcast_to((counts[tile] > 0).astype(jnp.int32), (8, dim))
            for j in range(3):
                meta_ref[b, 2 + j] = jnp.where(more > j, first + j, 7)


def pack(hidden_states, proj_weight, token_doc, token_live, start, nb):
    bl, d = hidden_states.shape[1:]
    dim = proj_weight.shape[1]
    return pl.pallas_call(
        functools.partial(pack_kernel, start=start),
        in_specs=[pl.BlockSpec(memory_space=pltpu.HBM)] * 4,
        out_specs=[VMEM, VMEM],
        out_shape=[
            pltpu.VMEM((nb, 128, dim), jnp.bfloat16),
            pltpu.VMEM((nb, 5, 8, dim), jnp.int32),
        ],
        scratch_shapes=[
            pltpu.VMEM((nb, bl, d), hidden_states.dtype),
            pltpu.VMEM((d, dim), proj_weight.dtype),
            pltpu.VMEM((nb, bl), jnp.int32),
            pltpu.VMEM((nb, bl), jnp.int32),
            pltpu.SemaphoreType.DMA((3 + nb // GROUP,)),
        ],
        cost_estimate=pl.CostEstimate(
            flops=2 * nb * bl * d * dim, bytes_accessed=2 * nb * bl * d, transcendentals=nb * bl
        ),
        compiler_params=PARAMS,
        name="pack",
    )(*(in_hbm(x) for x in (hidden_states, proj_weight, token_doc, token_live)))


def score_kernel(owner_ref, *refs, parts, width):
    vec_refs, meta_refs, got_ref = refs[:parts], refs[parts : 2 * parts], refs[2 * parts]
    keep_ref, send_ref, query_ref, table_ref = refs[2 * parts + 1 :]
    n = lax.axis_size("wide")
    bits = n.bit_length() - 1
    me = lax.axis_index("wide")
    columns = got_ref.shape[0]
    piece = columns // (n // 2)
    for j in range(n // 2):
        chip = (me >> 1) ^ bit_reverse(j, bits - 1)
        query_ref[pl.ds(pl.multiple_of(chip * piece, piece), piece), :] = got_ref[
            j * piece : (j + 1) * piece, :
        ]
    table_ref[...] = jnp.full(table_ref.shape, LOW, jnp.float32)
    span = min(columns, 512)

    def visit(vec_ref, meta_ref, b, offset, start):
        place = bit_reverse(owner_ref[offset + b] ^ me, bits)
        rows = pl.ds(pl.multiple_of(place * DOC_DEV, DOC_DEV), DOC_DEV)
        some = [meta_ref[b, tile] > 0 for tile in range(2)]
        index = [meta_ref[b, 2 + j] for j in range(3)]
        tokens = vec_ref[b]
        for t in range(span // width):
            at = pl.ds(start + t * width, width)
            similar = lax.dot_general(
                tokens,
                query_ref[at, :],
                (((1,), (1,)), ((), ())),
                preferred_element_type=jnp.float32,
            )
            first, rest = (
                functools.reduce(
                    jnp.maximum,
                    [similar[64 * tile + 8 * g : 64 * tile + 8 * g + 8] for g in range(CHUNK)],
                )
                for tile in range(2)
            )
            best = []
            for c in range(width // 128):
                top = jnp.where(some[0], first[:, c * 128 : (c + 1) * 128], LOW)
                further = jnp.where(some[1], rest[:, c * 128 : (c + 1) * 128], LOW)
                for j in range(3):
                    top = jnp.maximum(top, jnp.take_along_axis(further, index[j], axis=0))
                best.append(top)
            table_ref[rows, at] = jnp.maximum(table_ref[rows, at], jnp.concatenate(best, axis=1))

    def over_blocks(start):
        offset = 0
        for vec_ref, meta_ref in zip(vec_refs, meta_refs):
            nb = vec_ref.shape[0]
            step = next(s for s in (UNROLL, 12, 8, 4, 2, 1) if nb % s == 0)

            def some_blocks(i, carry, vec_ref=vec_ref, meta_ref=meta_ref, offset=offset, step=step):
                for u in range(step):
                    visit(vec_ref, meta_ref, i * step + u, offset, start)
                return carry

            lax.fori_loop(0, nb // step, some_blocks, 0)
            offset += nb

    if columns == span:
        over_blocks(0)
    else:

        def one_span(i, carry):
            over_blocks(pl.multiple_of(i * span, span))
            return carry

        lax.fori_loop(0, columns // span, one_span, 0)
    half = table_ref.shape[0] // 2
    keep_ref[...] = table_ref[:half, :]
    send_ref[...] = table_ref[half:, :]


def score(owner, packed, meta, gathered, owners):
    dim = gathered.shape[1]
    columns = gathered.shape[0]
    rows = sum(p.shape[0] * p.shape[1] for p in packed)
    half = pltpu.VMEM((owners * DOC_DEV // 2, columns), jnp.float32)
    return pl.pallas_call(
        functools.partial(score_kernel, parts=len(packed), width=256),
        in_specs=[pl.BlockSpec(memory_space=pltpu.SMEM)] + [VMEM] * (2 * len(packed) + 1),
        out_specs=[VMEM, VMEM],
        out_shape=[half, half],
        scratch_shapes=[
            pltpu.VMEM((columns, dim), jnp.bfloat16),
            pltpu.VMEM((owners * DOC_DEV, columns), jnp.float32),
        ],
        cost_estimate=pl.CostEstimate(
            flops=2 * rows * dim * columns, bytes_accessed=4 * rows * dim, transcendentals=0
        ),
        compiler_params=PARAMS,
    )(owner, *packed, *meta, in_vmem(gathered))


def in_hbm(x):
    return pltpu.with_memory_space_constraint(x, pltpu.HBM)


def in_vmem(x):
    return pltpu.with_memory_space_constraint(x, pltpu.VMEM)


def finish_kernel(keep_ref, got_ref, out_ref):
    best = jnp.maximum(keep_ref[...], got_ref[...])
    best = jnp.where(best > -100000000.0, best, jnp.float32(0.0))
    half = best.shape[1] // 2
    odd = (lax.axis_index("wide") & 1) == 1
    even_queries = jnp.where(odd, best[:, half:], best[:, :half])
    odd_queries = jnp.where(odd, best[:, :half], best[:, half:])
    low = lax.broadcasted_iota(jnp.int32, (best.shape[0], 128), 1) < 64
    for tile in range(half // 128):
        at = slice(tile * 128, (tile + 1) * 128)
        a, b = even_queries[:, at], odd_queries[:, at]
        out_ref[:, 2 * tile * 128 : (2 * tile + 1) * 128] = jnp.where(low, a, pltpu.roll(b, 64, 1))
        out_ref[:, (2 * tile + 1) * 128 : (2 * tile + 2) * 128] = jnp.where(low, pltpu.roll(a, 64, 1), b)


def finish(keep, got):
    return pl.pallas_call(
        finish_kernel,
        in_specs=[VMEM, VMEM],
        out_specs=VMEM,
        out_shape=jax.ShapeDtypeStruct(keep.shape, jnp.float32),
        compiler_params=PARAMS,
        name="finish",
    )(in_vmem(keep), in_vmem(got))


def program(hidden_states, block_owner, token_doc, token_live, proj_weight, queries):
    n = lax.axis_size("wide")
    nblocks = hidden_states.shape[0]
    if n & (n - 1) or queries.shape[0] != 64:
        raise ValueError("sizes")

    def swap(x, stride):
        return lax.ppermute(x, "wide", [(i, i ^ stride) for i in range(n)])

    strides = [1 << bit for bit in range(n.bit_length() - 1)]
    packed, meta, start = [], [], 0
    for share in PARTS:
        count = nblocks * share // sum(PARTS)
        vectors, layout = pack(hidden_states, proj_weight, token_doc, token_live, start, count)
        packed.append(vectors)
        meta.append(layout)
        start += count
    mine = queries
    for stride in reversed(strides[1:]):
        got = swap(mine, stride)
        mine = jnp.concatenate([mine, got], axis=0)
    other = swap(mine, 1)
    owner = block_owner.reshape(-1)
    keep_a, send_a = score(owner, packed, meta, mine, n)
    got_b = swap(send_a, 1)
    keep_b, send_b = score(owner, packed, meta, other, n)
    got_a = swap(send_b, 1)
    best = jnp.concatenate([jnp.maximum(keep_a, got_a), jnp.maximum(keep_b, got_b)], axis=1)
    for stride in strides[1:]:
        half = best.shape[0] // 2
        keep, got = best[:half], swap(best[half:], stride)
        if stride != strides[-1]:
            best = jnp.maximum(keep, got)
    return finish(keep, got)


def solution(mesh):
    placed = (
        P(("groups", "wide"), None, None),
        P(("groups", "wide"), None),
        P(("groups", "wide"), None),
        P(("groups", "wide"), None),
        P(),
        P(("groups", "wide"), None),
    )
    return jax.shard_map(program, mesh=mesh, in_specs=placed, out_specs=P(("groups", "wide"), None), check_vma=False)
```

```python
import functools

import jax
import jax.numpy as jnp
from jax import lax
from jax.experimental import pallas as pl
from jax.experimental.pallas import tpu as pltpu
from jax.sharding import PartitionSpec as P


DOC_DEV = 8
CHUNK = 8
GROUP = 8
UNROLL = 24
LOW = -1000000000.0
SENT = jnp.float16
SCALE = 4096.0
NONE = -60000.0
PARTS = (2, 3, 3)

VMEM = pl.BlockSpec(memory_space=pltpu.VMEM)
PARAMS = pltpu.CompilerParams(vmem_limit_bytes=24 << 20)


def bit_reverse(value, bits):
    out = value * 0
    for bit in range(bits):
        out = out | (((value >> bit) & 1) << (bits - 1 - bit))
    return out


def place_tokens(doc, live):
    nb, bl = doc.shape
    livef = live.astype(jnp.float32)
    upto = lax.broadcasted_iota(jnp.int32, (bl, bl), 0) <= lax.broadcasted_iota(
        jnp.int32, (bl, bl), 1
    )
    counted = jnp.dot(livef, upto.astype(jnp.float32), preferred_element_type=jnp.float32)
    before = jnp.zeros((nb, bl), jnp.float32)
    extra = jnp.zeros((nb, bl), jnp.int32)
    for slot in range(DOC_DEV):
        n = jnp.sum(jnp.where(doc == slot, livef, 0.0), axis=1, keepdims=True)
        more = jnp.maximum((n.astype(jnp.int32) - 1) >> 3, 0)
        before = before + jnp.where(doc > slot, n, 0.0)
        extra = extra + jnp.where(doc > slot, more, 0)
    rank = (counted - livef - before).astype(jnp.int32)
    part, group = rank >> 3, rank & 7
    row = jnp.where(part == 0, group * 8 + doc, 64 + group * 8 + extra + part - 1)
    return jnp.where(live, row, -1), jnp.where(live, doc, -1)


def pack_blocks(project, groups, w_ref, row_ref, doc_ref, start, out_ref, meta_ref):
    bl = row_ref.shape[1]
    dim = w_ref.shape[1]
    sub = lax.broadcasted_iota(jnp.int32, (8, bl), 0)
    earlier = (
        lax.broadcasted_iota(jnp.int32, (8, 8), 0) > lax.broadcasted_iota(jnp.int32, (8, 8), 1)
    ).astype(jnp.float32)
    coming = project(0)
    for g in range(groups):
        vectors = coming
        if g + 1 < groups:
            coming = project(g + 1)
        for u in range(GROUP):
            b = g * GROUP + u
            row = row_ref[start + b : start + b + 1, :]
            tiles, counts = [], []
            for tile in range(2):
                hits = [
                    (row == sub + (64 * tile + 8 * i)).astype(jnp.float32) for i in range(CHUNK)
                ]
                count = jnp.sum(functools.reduce(jnp.add, hits), axis=1, keepdims=True)
                counts.append(count)
                tiles += hits[:1]
                tiles += [jnp.where(count > float(i), hits[i], hits[0]) for i in range(1, CHUNK)]
            pick = jnp.concatenate(tiles, axis=0).astype(jnp.bfloat16)
            out_ref[b] = jnp.dot(
                pick, vectors[u * bl : (u + 1) * bl], preferred_element_type=jnp.float32
            ).astype(jnp.bfloat16)
            doc = doc_ref[start + b : start + b + 1, :]
            n = jnp.sum((doc == sub).astype(jnp.float32), axis=1, keepdims=True)
            n = jnp.broadcast_to(n, (8, dim)).astype(jnp.int32)
            more = jnp.maximum((n - 1) >> 3, 0)
            first = jnp.dot(
                earlier, more.astype(jnp.float32), preferred_element_type=jnp.float32
            ).astype(jnp.int32)
            for tile in range(2):
                meta_ref[b, tile] = jnp.broadcast_to((counts[tile] > 0).astype(jnp.int32), (8, dim))
            for j in range(3):
                meta_ref[b, 2 + j] = jnp.where(more > j, first + j, 7)


def vectors_of(h, w):
    projected = jnp.dot(h.reshape(-1, h.shape[-1]), w, preferred_element_type=jnp.float32)
    total = jnp.sum(projected * projected, axis=1, keepdims=True)
    return (projected * lax.rsqrt(total + 1e-06)).astype(jnp.bfloat16)


def pack_first_kernel(
    h_hbm, w_hbm, doc_hbm, live_hbm, out_ref, meta_ref, next_ref, w_ref, row_ref, doc_ref, *scratch
):
    h_ref, token_ref, live_ref, sems = scratch
    nb, count = h_ref.shape[0], next_ref.shape[0]
    groups = nb // GROUP
    small = [
        pltpu.make_async_copy(doc_hbm, token_ref, sems.at[0]),
        pltpu.make_async_copy(live_hbm, live_ref, sems.at[1]),
        pltpu.make_async_copy(w_hbm, w_ref, sems.at[2]),
    ]
    large = [
        pltpu.make_async_copy(
            h_hbm.at[pl.ds(g * GROUP, GROUP)], h_ref.at[pl.ds(g * GROUP, GROUP)], sems.at[4 + g]
        )
        for g in range(groups)
    ]
    later = pltpu.make_async_copy(h_hbm.at[pl.ds(nb, count)], next_ref, sems.at[3])
    for copy in small + large + [later]:
        copy.start()
    small[0].wait()
    small[1].wait()
    row, doc = place_tokens(token_ref[...], live_ref[...] == 1)
    row_ref[...] = row
    doc_ref[...] = doc
    small[2].wait()

    def project(g):
        large[g].wait()
        return vectors_of(h_ref[g * GROUP : (g + 1) * GROUP], w_ref[...])

    pack_blocks(project, groups, w_ref, row_ref, doc_ref, 0, out_ref, meta_ref)
    later.wait()


def pack_next_kernel(h_ref, w_ref, row_ref, doc_ref, *refs, start, more):
    nb = h_ref.shape[0]
    if more:
        h_hbm, out_ref, meta_ref, next_ref, sem = refs
        later = pltpu.make_async_copy(
            h_hbm.at[pl.ds(start + nb, next_ref.shape[0])], next_ref, sem.at[0]
        )
        later.start()
    else:
        out_ref, meta_ref = refs

    def project(g):
        return vectors_of(h_ref[g * GROUP : (g + 1) * GROUP], w_ref[...])

    pack_blocks(project, nb // GROUP, w_ref, row_ref, doc_ref, start, out_ref, meta_ref)
    if more:
        later.wait()


def pack(hidden_states, proj_weight, token_doc, token_live):
    nblocks, bl, d = hidden_states.shape
    dim = proj_weight.shape[1]
    sizes = [nblocks * share // sum(PARTS) for share in PARTS]
    starts = [sum(sizes[:i]) for i in range(len(sizes))]
    hidden = in_hbm(hidden_states)

    def outputs(i):
        shapes = [
            pltpu.VMEM((sizes[i], 128, dim), jnp.bfloat16),
            pltpu.VMEM((sizes[i], 5, 8, dim), jnp.int32),
        ]
        if i + 1 < len(sizes):
            shapes.append(pltpu.VMEM((sizes[i + 1], bl, d), hidden_states.dtype))
        return shapes

    def cost(i):
        tokens = sizes[i] * bl
        return pl.CostEstimate(
            flops=2 * tokens * d * dim, bytes_accessed=2 * tokens * d, transcendentals=tokens
        )

    def first():
        shapes = outputs(0) + [
            pltpu.VMEM((d, dim), proj_weight.dtype),
            pltpu.VMEM((nblocks, bl), jnp.int32),
            pltpu.VMEM((nblocks, bl), jnp.int32),
        ]
        return pl.pallas_call(
            pack_first_kernel,
            in_specs=[pl.BlockSpec(memory_space=pltpu.HBM)] * 4,
            out_specs=[VMEM] * len(shapes),
            out_shape=shapes,
            scratch_shapes=[
                pltpu.VMEM((sizes[0], bl, d), hidden_states.dtype),
                pltpu.VMEM((nblocks, bl), jnp.int32),
                pltpu.VMEM((nblocks, bl), jnp.int32),
                pltpu.SemaphoreType.DMA((4 + sizes[0] // GROUP,)),
            ],
            cost_estimate=cost(0),
            compiler_params=PARAMS,
            name="pack_first",
        )(hidden, *(in_hbm(x) for x in (proj_weight, token_doc, token_live)))

    def following(i, fetched, weight, row, doc):
        more = i + 1 < len(sizes)
        return pl.pallas_call(
            functools.partial(pack_next_kernel, start=starts[i], more=more),
            in_specs=[VMEM] * 4 + [pl.BlockSpec(memory_space=pltpu.HBM)] * more,
            out_specs=[VMEM] * (3 if more else 2),
            out_shape=outputs(i),
            scratch_shapes=[pltpu.SemaphoreType.DMA((1,))] * more,
            cost_estimate=cost(i),
            compiler_params=PARAMS,
            name="pack_next",
        )(fetched, weight, row, doc, *[hidden] * more)

    packed, meta = [], []
    for i in range(len(sizes)):
        if i == 0:
            vectors, layout, *left, weight, row, doc = first()
        else:
            vectors, layout, *left = following(i, left[0], weight, row, doc)
        packed.append(vectors)
        meta.append(layout)
    return packed, meta


def score_kernel(owner_ref, *refs, parts, pieces, width):
    vec_refs, meta_refs = refs[:parts], refs[parts : 2 * parts]
    got_refs = refs[2 * parts : 2 * parts + pieces]
    keep_ref, send_ref, unit_ref, query_ref, table_ref = refs[2 * parts + pieces :]
    n = lax.axis_size("wide")
    bits = n.bit_length() - 1
    me = lax.axis_index("wide")
    columns = query_ref.shape[0]
    piece = columns // (n // 2)
    largest = jnp.zeros((16, query_ref.shape[1]), jnp.float32)
    j = 0
    for got_ref in got_refs:
        for k in range(got_ref.shape[0] // piece):
            chip = (me >> 1) ^ bit_reverse(j, bits - 1)
            block = got_ref[k * piece : (k + 1) * piece, :]
            query_ref[pl.ds(pl.multiple_of(chip * piece, piece), piece), :] = block
            size = jnp.abs(block.astype(jnp.float32))
            for r in range(0, piece, 16):
                largest = jnp.maximum(largest, size[r : r + 16])
            j += 1
    unit = jnp.max(jnp.max(largest, axis=1, keepdims=True), axis=0, keepdims=True)
    unit = jnp.broadcast_to(jnp.where(unit > 0.0, unit, 1.0) * (1.0 / SCALE), unit_ref.shape)
    unit_ref[...] = unit
    table_ref[...] = jnp.full(table_ref.shape, LOW, jnp.float32)
    span = min(columns, 512)

    def visit(vec_ref, meta_ref, b, offset, start):
        place = bit_reverse(owner_ref[offset + b] ^ me, bits)
        rows = pl.ds(pl.multiple_of(place * DOC_DEV, DOC_DEV), DOC_DEV)
        some = [meta_ref[b, tile] > 0 for tile in range(2)]
        index = [meta_ref[b, 2 + j] for j in range(3)]
        tokens = vec_ref[b]
        for t in range(span // width):
            at = pl.ds(start + t * width, width)
            similar = lax.dot_general(
                tokens,
                query_ref[at, :],
                (((1,), (1,)), ((), ())),
                preferred_element_type=jnp.float32,
            )
            first, rest = (
                functools.reduce(
                    jnp.maximum,
                    [similar[64 * tile + 8 * g : 64 * tile + 8 * g + 8] for g in range(CHUNK)],
                )
                for tile in range(2)
            )
            best = []
            for c in range(width // 128):
                top = jnp.where(some[0], first[:, c * 128 : (c + 1) * 128], LOW)
                further = jnp.where(some[1], rest[:, c * 128 : (c + 1) * 128], LOW)
                for j in range(3):
                    top = jnp.maximum(top, jnp.take_along_axis(further, index[j], axis=0))
                best.append(top)
            table_ref[rows, at] = jnp.maximum(table_ref[rows, at], jnp.concatenate(best, axis=1))

    def over_blocks(start):
        offset = 0
        for vec_ref, meta_ref in zip(vec_refs, meta_refs):
            nb = vec_ref.shape[0]
            step = next(s for s in (UNROLL, 16, 8, 4, 2, 1) if nb % s == 0)

            def some_blocks(i, carry, vec_ref=vec_ref, meta_ref=meta_ref, offset=offset, step=step):
                for u in range(step):
                    visit(vec_ref, meta_ref, i * step + u, offset, start)
                return carry

            lax.fori_loop(0, nb // step, some_blocks, 0)
            offset += nb

    if columns == span:
        over_blocks(0)
    else:

        def one_span(i, carry):
            over_blocks(pl.multiple_of(i * span, span))
            return carry

        lax.fori_loop(0, columns // span, one_span, 0)
    half = table_ref.shape[0] // 2
    factor = 1.0 / unit[:1, :1]
    keep_ref[...] = jnp.maximum(table_ref[:half, :] * factor, NONE)
    send_ref[...] = jnp.maximum(table_ref[half:, :] * factor, NONE)


def score(owner, packed, meta, gathered, owners):
    dim = gathered[0].shape[1]
    columns = sum(piece.shape[0] for piece in gathered)
    rows = sum(p.shape[0] * p.shape[1] for p in packed)
    half = (owners * DOC_DEV // 2, columns)
    return pl.pallas_call(
        functools.partial(score_kernel, parts=len(packed), pieces=len(gathered), width=256),
        in_specs=[pl.BlockSpec(memory_space=pltpu.SMEM)] + [VMEM] * (2 * len(packed) + len(gathered)),
        out_specs=[VMEM] * 3,
        out_shape=[
            pltpu.VMEM(half, jnp.float32),
            pltpu.VMEM(half, jnp.float32),
            pltpu.VMEM((8, 128), jnp.float32),
        ],
        scratch_shapes=[
            pltpu.VMEM((columns, dim), jnp.bfloat16),
            pltpu.VMEM((owners * DOC_DEV, columns), jnp.float32),
        ],
        cost_estimate=pl.CostEstimate(
            flops=2 * rows * dim * columns, bytes_accessed=4 * rows * dim, transcendentals=0
        ),
        compiler_params=PARAMS,
    )(owner, *packed, *meta, *(in_vmem(x) for x in gathered))


def in_hbm(x):
    return pltpu.with_memory_space_constraint(x, pltpu.HBM)


def in_vmem(x):
    return pltpu.with_memory_space_constraint(x, pltpu.VMEM)


def finish_kernel(keep_ref, got_ref, unit_a_ref, unit_b_ref, out_ref):
    best = jnp.maximum(keep_ref[...], got_ref[...])
    half = best.shape[1] // 2
    best = jnp.where(best > 0.9 * NONE, best, 0.0)
    best = jnp.concatenate(
        [best[:, :half] * unit_a_ref[:1, :1], best[:, half:] * unit_b_ref[:1, :1]], axis=1
    )
    odd = (lax.axis_index("wide") & 1) == 1
    even_queries = jnp.where(odd, best[:, half:], best[:, :half])
    odd_queries = jnp.where(odd, best[:, :half], best[:, half:])
    low = lax.broadcasted_iota(jnp.int32, (best.shape[0], 128), 1) < 64
    for tile in range(half // 128):
        at = slice(tile * 128, (tile + 1) * 128)
        a, b = even_queries[:, at], odd_queries[:, at]
        out_ref[:, 2 * tile * 128 : (2 * tile + 1) * 128] = jnp.where(low, a, pltpu.roll(b, 64, 1))
        out_ref[:, (2 * tile + 1) * 128 : (2 * tile + 2) * 128] = jnp.where(low, pltpu.roll(a, 64, 1), b)


def finish(keep, got, unit_a, unit_b):
    return pl.pallas_call(
        finish_kernel,
        in_specs=[VMEM] * 4,
        out_specs=VMEM,
        out_shape=jax.ShapeDtypeStruct(keep.shape, jnp.float32),
        compiler_params=PARAMS,
        name="finish",
    )(*(in_vmem(x) for x in (keep, got, unit_a, unit_b)))


def program(hidden_states, block_owner, token_doc, token_live, proj_weight, queries):
    n = lax.axis_size("wide")
    if n & (n - 1) or queries.shape[0] != 64:
        raise ValueError("sizes")

    def swap(x, stride):
        return lax.ppermute(x, "wide", [(i, i ^ stride) for i in range(n)])

    strides = [1 << bit for bit in range(n.bit_length() - 1)]
    packed, meta = pack(hidden_states, proj_weight, token_doc, token_live)
    pieces, mine = [queries], queries
    for stride in reversed(strides[1:]):
        pieces.append(swap(mine, stride))
        mine = lax.optimization_barrier(jnp.concatenate([mine, pieces[-1]], axis=0))
    other = swap(mine, 1)
    owner = block_owner.reshape(-1)
    keep_a, send_a, unit_a = score(owner, packed, meta, pieces, n)
    got_b = swap(send_a.astype(SENT), 1)
    keep_b, send_b, unit_b = score(owner, packed, meta, [other], n)
    got_a = swap(send_b.astype(SENT), 1)
    best = jnp.concatenate(
        [
            jnp.maximum(keep_a, got_a.astype(jnp.float32)),
            jnp.maximum(keep_b, got_b.astype(jnp.float32)),
        ],
        axis=1,
    )
    for stride in strides[1:]:
        half = best.shape[0] // 2
        keep, got = best[:half], swap(best[half:].astype(SENT), stride)
        if stride != strides[-1]:
            best = jnp.maximum(keep, got.astype(jnp.float32))
    return finish(keep, got.astype(jnp.float32), unit_a, unit_b)


def solution(mesh):
    placed = (
        P(("groups", "wide"), None, None),
        P(("groups", "wide"), None),
        P(("groups", "wide"), None),
        P(("groups", "wide"), None),
        P(),
        P(("groups", "wide"), None),
    )
    return jax.shard_map(
        program, mesh=mesh, in_specs=placed, out_specs=P(("groups", "wide"), None), check_vma=False
    )
```

```python
import functools

import jax
import jax.numpy as jnp
from jax import lax
from jax.experimental import pallas as pl
from jax.experimental.pallas import tpu as pltpu
from jax.sharding import PartitionSpec as P


DOC_DEV = 8
CHUNK = 8
GROUP = 8
UNROLL = 24
LOW = -1000000000.0
SENT = jnp.float16
SCALE = 4096.0
NONE = -60000.0
PARTS = (1, 3, 4)

VMEM = pl.BlockSpec(memory_space=pltpu.VMEM)
PARAMS = pltpu.CompilerParams(vmem_limit_bytes=24 << 20)


def bit_reverse(value, bits):
    out = value * 0
    for bit in range(bits):
        out = out | (((value >> bit) & 1) << (bits - 1 - bit))
    return out


def parity(value, bits):
    out = value * 0
    for bit in range(bits):
        out = out ^ ((value >> bit) & 1)
    return out


def once(body):
    def run(i, carry):
        body()
        return carry

    lax.fori_loop(0, 1 + (lax.axis_index("wide") >> 20), run, 0)


def place_tokens(doc, live):
    nb, bl = doc.shape
    livef = live.astype(jnp.float32)
    upto = lax.broadcasted_iota(jnp.int32, (bl, bl), 0) <= lax.broadcasted_iota(
        jnp.int32, (bl, bl), 1
    )
    counted = jnp.dot(livef, upto.astype(jnp.float32), preferred_element_type=jnp.float32)
    before = jnp.zeros((nb, bl), jnp.float32)
    extra = jnp.zeros((nb, bl), jnp.int32)
    for slot in range(DOC_DEV):
        n = jnp.sum(jnp.where(doc == slot, livef, 0.0), axis=1, keepdims=True)
        more = jnp.maximum((n.astype(jnp.int32) - 1) >> 3, 0)
        before = before + jnp.where(doc > slot, n, 0.0)
        extra = extra + jnp.where(doc > slot, more, 0)
    rank = (counted - livef - before).astype(jnp.int32)
    part, group = rank >> 3, rank & 7
    row = jnp.where(part == 0, group * 8 + doc, 64 + group * 8 + extra + part - 1)
    return jnp.where(live, row, -1), jnp.where(live, doc, -1)


def pack_blocks(project, groups, w_ref, row_ref, doc_ref, start, out_ref, meta_ref):
    bl = row_ref.shape[1]
    dim = w_ref.shape[1]
    sub = lax.broadcasted_iota(jnp.int32, (8, bl), 0)
    earlier = (
        lax.broadcasted_iota(jnp.int32, (8, 8), 0) > lax.broadcasted_iota(jnp.int32, (8, 8), 1)
    ).astype(jnp.float32)
    coming = project(0)
    for g in range(groups):
        vectors = coming
        if g + 1 < groups:
            coming = project(g + 1)
        for u in range(GROUP):
            b = g * GROUP + u
            row = row_ref[start + b : start + b + 1, :]
            tiles, counts = [], []
            for tile in range(2):
                hits = [
                    (row == sub + (64 * tile + 8 * i)).astype(jnp.float32) for i in range(CHUNK)
                ]
                count = jnp.sum(functools.reduce(jnp.add, hits), axis=1, keepdims=True)
                counts.append(count)
                tiles += hits[:1]
                tiles += [jnp.where(count > float(i), hits[i], hits[0]) for i in range(1, CHUNK)]
            pick = jnp.concatenate(tiles, axis=0).astype(jnp.bfloat16)
            out_ref[b] = jnp.dot(
                pick, vectors[u * bl : (u + 1) * bl], preferred_element_type=jnp.float32
            ).astype(jnp.bfloat16)
            doc = doc_ref[start + b : start + b + 1, :]
            n = jnp.sum((doc == sub).astype(jnp.float32), axis=1, keepdims=True)
            n = jnp.broadcast_to(n, (8, dim)).astype(jnp.int32)
            more = jnp.maximum((n - 1) >> 3, 0)
            first = jnp.dot(
                earlier, more.astype(jnp.float32), preferred_element_type=jnp.float32
            ).astype(jnp.int32)
            for tile in range(2):
                meta_ref[b, tile] = jnp.broadcast_to((counts[tile] > 0).astype(jnp.int32), (8, dim))
            for j in range(3):
                meta_ref[b, 2 + j] = jnp.where(more > j, first + j, 7)


def vectors_of(h, w):
    projected = jnp.dot(h.reshape(-1, h.shape[-1]), w, preferred_element_type=jnp.float32)
    total = jnp.sum(projected * projected, axis=1, keepdims=True)
    return (projected * lax.rsqrt(total + 1e-06)).astype(jnp.bfloat16)


def pack_first_kernel(
    h_hbm, w_hbm, doc_hbm, live_hbm, out_ref, meta_ref, next_ref, w_ref, row_ref, doc_ref, *scratch
):
    h_ref, token_ref, live_ref, sems = scratch
    nb, count = h_ref.shape[0], next_ref.shape[0]
    groups = nb // GROUP
    small = [
        pltpu.make_async_copy(doc_hbm, token_ref, sems.at[0]),
        pltpu.make_async_copy(live_hbm, live_ref, sems.at[1]),
        pltpu.make_async_copy(w_hbm, w_ref, sems.at[2]),
    ]
    large = [
        pltpu.make_async_copy(
            h_hbm.at[pl.ds(g * GROUP, GROUP)], h_ref.at[pl.ds(g * GROUP, GROUP)], sems.at[4 + g]
        )
        for g in range(groups)
    ]
    later = pltpu.make_async_copy(h_hbm.at[pl.ds(nb, count)], next_ref, sems.at[3])
    for copy in small + large + [later]:
        copy.start()
    small[0].wait()
    small[1].wait()
    row, doc = place_tokens(token_ref[...], live_ref[...] == 1)
    row_ref[...] = row
    doc_ref[...] = doc
    small[2].wait()
    for copy in large:
        copy.wait()

    def project(g):
        return vectors_of(h_ref[g * GROUP : (g + 1) * GROUP], w_ref[...])

    once(lambda: pack_blocks(project, groups, w_ref, row_ref, doc_ref, 0, out_ref, meta_ref))
    later.wait()


def pack_next_kernel(h_ref, w_ref, row_ref, doc_ref, *refs, start, more):
    nb = h_ref.shape[0]
    if more:
        h_hbm, out_ref, meta_ref, next_ref, sem = refs
        later = pltpu.make_async_copy(
            h_hbm.at[pl.ds(start + nb, next_ref.shape[0])], next_ref, sem.at[0]
        )
        later.start()
    else:
        out_ref, meta_ref = refs

    def project(g):
        return vectors_of(h_ref[g * GROUP : (g + 1) * GROUP], w_ref[...])

    groups = nb // GROUP
    once(lambda: pack_blocks(project, groups, w_ref, row_ref, doc_ref, start, out_ref, meta_ref))
    if more:
        later.wait()


def pack(hidden_states, proj_weight, token_doc, token_live):
    nblocks, bl, d = hidden_states.shape
    dim = proj_weight.shape[1]
    sizes = [nblocks * share // sum(PARTS) for share in PARTS]
    starts = [sum(sizes[:i]) for i in range(len(sizes))]
    hidden = in_hbm(hidden_states)

    def outputs(i):
        shapes = [
            pltpu.VMEM((sizes[i], 128, dim), jnp.bfloat16),
            pltpu.VMEM((sizes[i], 5, 8, dim), jnp.int32),
        ]
        if i + 1 < len(sizes):
            shapes.append(pltpu.VMEM((sizes[i + 1], bl, d), hidden_states.dtype))
        return shapes

    def cost(i):
        tokens = sizes[i] * bl
        return pl.CostEstimate(
            flops=2 * tokens * d * dim, bytes_accessed=2 * tokens * d, transcendentals=tokens
        )

    def first():
        shapes = outputs(0) + [
            pltpu.VMEM((d, dim), proj_weight.dtype),
            pltpu.VMEM((nblocks, bl), jnp.int32),
            pltpu.VMEM((nblocks, bl), jnp.int32),
        ]
        return pl.pallas_call(
            pack_first_kernel,
            in_specs=[pl.BlockSpec(memory_space=pltpu.HBM)] * 4,
            out_specs=[VMEM] * len(shapes),
            out_shape=shapes,
            scratch_shapes=[
                pltpu.VMEM((sizes[0], bl, d), hidden_states.dtype),
                pltpu.VMEM((nblocks, bl), jnp.int32),
                pltpu.VMEM((nblocks, bl), jnp.int32),
                pltpu.SemaphoreType.DMA((4 + sizes[0] // GROUP,)),
            ],
            cost_estimate=cost(0),
            compiler_params=PARAMS,
            name="pack_first",
        )(hidden, *(in_hbm(x) for x in (proj_weight, token_doc, token_live)))

    def following(i, fetched, weight, row, doc):
        more = i + 1 < len(sizes)
        return pl.pallas_call(
            functools.partial(pack_next_kernel, start=starts[i], more=more),
            in_specs=[VMEM] * 4 + [pl.BlockSpec(memory_space=pltpu.HBM)] * more,
            out_specs=[VMEM] * (3 if more else 2),
            out_shape=outputs(i),
            scratch_shapes=[pltpu.SemaphoreType.DMA((1,))] * more,
            cost_estimate=cost(i),
            compiler_params=PARAMS,
            name="pack_next",
        )(fetched, weight, row, doc, *[hidden] * more)

    packed, meta = [], []
    for i in range(len(sizes)):
        if i == 0:
            vectors, layout, *left, weight, row, doc = first()
        else:
            vectors, layout, *left = following(i, left[0], weight, row, doc)
        packed.append(vectors)
        meta.append(layout)
    return packed, meta


def score_kernel(owner_ref, *refs, parts, pieces, width):
    vec_refs, meta_refs = refs[:parts], refs[parts : 2 * parts]
    got_refs = refs[2 * parts : 2 * parts + pieces]
    keep_ref, send_ref, unit_ref, query_ref, table_ref = refs[2 * parts + pieces :]
    n = lax.axis_size("wide")
    bits = n.bit_length() - 1
    me = lax.axis_index("wide")
    columns = query_ref.shape[0]
    piece = columns // (n // 2)
    largest = jnp.zeros((16, query_ref.shape[1]), jnp.float32)
    j = 0
    for got_ref in got_refs:
        for k in range(got_ref.shape[0] // piece):
            chip = (me >> 1) ^ bit_reverse(j, bits - 1)
            block = got_ref[k * piece : (k + 1) * piece, :]
            query_ref[pl.ds(pl.multiple_of(chip * piece, piece), piece), :] = block
            size = jnp.abs(block.astype(jnp.float32))
            for r in range(0, piece, 16):
                largest = jnp.maximum(largest, size[r : r + 16])
            j += 1
    unit = jnp.max(jnp.max(largest, axis=1, keepdims=True), axis=0, keepdims=True)
    unit = jnp.broadcast_to(jnp.where(unit > 0.0, unit, 1.0) * (1.0 / SCALE), unit_ref.shape)
    unit_ref[...] = unit
    table_ref[...] = jnp.full(table_ref.shape, LOW, jnp.float32)
    span = min(columns, 512)

    def visit(vec_ref, meta_ref, b, offset, start):
        apart = owner_ref[offset + b] ^ me
        place = (parity(apart, bits) << (bits - 1)) | bit_reverse(apart >> 1, bits - 1)
        rows = pl.ds(pl.multiple_of(place * DOC_DEV, DOC_DEV), DOC_DEV)
        some = [meta_ref[b, tile] > 0 for tile in range(2)]
        index = [meta_ref[b, 2 + j] for j in range(3)]
        tokens = vec_ref[b]
        for t in range(span // width):
            at = pl.ds(start + t * width, width)
            similar = lax.dot_general(
                tokens,
                query_ref[at, :],
                (((1,), (1,)), ((), ())),
                preferred_element_type=jnp.float32,
            )
            first, rest = (
                functools.reduce(
                    jnp.maximum,
                    [similar[64 * tile + 8 * g : 64 * tile + 8 * g + 8] for g in range(CHUNK)],
                )
                for tile in range(2)
            )
            best = []
            for c in range(width // 128):
                top = jnp.where(some[0], first[:, c * 128 : (c + 1) * 128], LOW)
                further = jnp.where(some[1], rest[:, c * 128 : (c + 1) * 128], LOW)
                for j in range(3):
                    top = jnp.maximum(top, jnp.take_along_axis(further, index[j], axis=0))
                best.append(top)
            table_ref[rows, at] = jnp.maximum(table_ref[rows, at], jnp.concatenate(best, axis=1))

    def over_blocks(start):
        offset = 0
        for vec_ref, meta_ref in zip(vec_refs, meta_refs):
            nb = vec_ref.shape[0]
            step = next(s for s in (UNROLL, 16, 8, 4, 2, 1) if nb % s == 0)

            def some_blocks(i, carry, vec_ref=vec_ref, meta_ref=meta_ref, offset=offset, step=step):
                for u in range(step):
                    visit(vec_ref, meta_ref, i * step + u, offset, start)
                return carry

            lax.fori_loop(0, nb // step, some_blocks, 0)
            offset += nb

    if columns == span:
        over_blocks(0)
    else:

        def one_span(i, carry):
            over_blocks(pl.multiple_of(i * span, span))
            return carry

        lax.fori_loop(0, columns // span, one_span, 0)
    half = table_ref.shape[0] // 2
    factor = 1.0 / unit[:1, :1]
    keep_ref[...] = jnp.maximum(table_ref[:half, :] * factor, NONE)
    send_ref[...] = jnp.maximum(table_ref[half:, :] * factor, NONE)


def score(owner, packed, meta, gathered, owners):
    dim = gathered[0].shape[1]
    columns = sum(piece.shape[0] for piece in gathered)
    rows = sum(p.shape[0] * p.shape[1] for p in packed)
    half = (owners * DOC_DEV // 2, columns)
    return pl.pallas_call(
        functools.partial(score_kernel, parts=len(packed), pieces=len(gathered), width=256),
        in_specs=[pl.BlockSpec(memory_space=pltpu.SMEM)] + [VMEM] * (2 * len(packed) + len(gathered)),
        out_specs=[VMEM] * 3,
        out_shape=[
            pltpu.VMEM(half, jnp.float32),
            pltpu.VMEM(half, jnp.float32),
            pltpu.VMEM((8, 128), jnp.float32),
        ],
        scratch_shapes=[
            pltpu.VMEM((columns, dim), jnp.bfloat16),
            pltpu.VMEM((owners * DOC_DEV, columns), jnp.float32),
        ],
        cost_estimate=pl.CostEstimate(
            flops=2 * rows * dim * columns, bytes_accessed=4 * rows * dim, transcendentals=0
        ),
        compiler_params=PARAMS,
    )(owner, *packed, *meta, *(in_vmem(x) for x in gathered))


def in_hbm(x):
    return pltpu.with_memory_space_constraint(x, pltpu.HBM)


def in_vmem(x):
    return pltpu.with_memory_space_constraint(x, pltpu.VMEM)


def finish_kernel(keep_ref, got_ref, unit_a_ref, unit_b_ref, out_ref):
    best = jnp.maximum(keep_ref[...], got_ref[...])
    half = best.shape[1] // 2
    best = jnp.where(best > 0.9 * NONE, best, 0.0)
    best = jnp.concatenate(
        [best[:, :half] * unit_a_ref[:1, :1], best[:, half:] * unit_b_ref[:1, :1]], axis=1
    )
    bits = lax.axis_size("wide").bit_length() - 1
    odd = parity(lax.axis_index("wide"), bits) == 1
    even_queries = jnp.where(odd, best[:, half:], best[:, :half])
    odd_queries = jnp.where(odd, best[:, :half], best[:, half:])
    low = lax.broadcasted_iota(jnp.int32, (best.shape[0], 128), 1) < 64
    for chip in range(half // 64):
        at = slice(chip // 2 * 128, chip // 2 * 128 + 128)
        a, b = even_queries[:, at], odd_queries[:, at]
        if parity(chip, bits):
            a, b = b, a
        if chip % 2:
            a = pltpu.roll(a, 64, 1)
        else:
            b = pltpu.roll(b, 64, 1)
        out_ref[:, chip * 128 : (chip + 1) * 128] = jnp.where(low, a, b)


def finish(keep, got, unit_a, unit_b):
    return pl.pallas_call(
        finish_kernel,
        in_specs=[VMEM] * 4,
        out_specs=VMEM,
        out_shape=jax.ShapeDtypeStruct(keep.shape, jnp.float32),
        compiler_params=PARAMS,
        name="finish",
    )(*(in_vmem(x) for x in (keep, got, unit_a, unit_b)))


def program(hidden_states, block_owner, token_doc, token_live, proj_weight, queries):
    n = lax.axis_size("wide")
    if n & (n - 1) or queries.shape[0] != 64:
        raise ValueError("sizes")

    def swap(x, stride):
        return lax.ppermute(x, "wide", [(i, i ^ stride) for i in range(n)])

    strides = [1] + [(1 << bit) | 1 for bit in range(1, n.bit_length() - 1)]
    packed, meta = pack(hidden_states, proj_weight, token_doc, token_live)
    pieces, mine = [queries], queries
    for stride in reversed(strides[1:]):
        pieces.append(swap(mine, stride))
        mine = lax.optimization_barrier(jnp.concatenate([mine, pieces[-1]], axis=0))
    other = swap(mine, 1)
    owner = block_owner.reshape(-1)
    keep_a, send_a, unit_a = score(owner, packed, meta, pieces, n)
    got_b = swap(send_a.astype(SENT), 1)
    keep_b, send_b, unit_b = score(owner, packed, meta, [other], n)
    got_a = swap(send_b.astype(SENT), 1)
    best = jnp.concatenate(
        [
            jnp.maximum(keep_a, got_a.astype(jnp.float32)),
            jnp.maximum(keep_b, got_b.astype(jnp.float32)),
        ],
        axis=1,
    )
    for stride in strides[1:]:
        half = best.shape[0] // 2
        keep, got = best[:half], swap(best[half:].astype(SENT), stride)
        if stride != strides[-1]:
            best = jnp.maximum(keep, got.astype(jnp.float32))
    return finish(keep, got.astype(jnp.float32), unit_a, unit_b)


def solution(mesh):
    placed = (
        P(("groups", "wide"), None, None),
        P(("groups", "wide"), None),
        P(("groups", "wide"), None),
        P(("groups", "wide"), None),
        P(),
        P(("groups", "wide"), None),
    )
    return jax.shard_map(
        program, mesh=mesh, in_specs=placed, out_specs=P(("groups", "wide"), None), check_vma=False
    )
```

```python
import functools

import jax
import jax.numpy as jnp
from jax import lax
from jax.experimental import pallas as pl
from jax.experimental.pallas import tpu as pltpu
from jax.sharding import PartitionSpec as P


DOC_DEV = 8
CHUNK = 7
ROWS = 2 * CHUNK * DOC_DEV
FURTHER = 4
GROUP = 8
UNROLL = 32
LOW = -1000000000.0
SENT = jnp.float16
SCALE = 4096.0
NONE = -60000.0
PARTS = (1, 3, 4)

VMEM = pl.BlockSpec(memory_space=pltpu.VMEM)
PARAMS = pltpu.CompilerParams(vmem_limit_bytes=24 << 20)


def bit_reverse(value, bits):
    out = value * 0
    for bit in range(bits):
        out = out | (((value >> bit) & 1) << (bits - 1 - bit))
    return out


def parity(value, bits):
    out = value * 0
    for bit in range(bits):
        out = out ^ ((value >> bit) & 1)
    return out


def chunks(value):
    return (value * 37) >> 8


def once(body):
    def run(i, carry):
        body()
        return carry

    lax.fori_loop(0, 1 + (lax.axis_index("wide") >> 20), run, 0)


def place_tokens(doc, live):
    nb, bl = doc.shape
    livef = live.astype(jnp.float32)
    upto = lax.broadcasted_iota(jnp.int32, (bl, bl), 0) <= lax.broadcasted_iota(
        jnp.int32, (bl, bl), 1
    )
    counted = jnp.dot(livef, upto.astype(jnp.float32), preferred_element_type=jnp.float32)
    before = jnp.zeros((nb, bl), jnp.float32)
    extra = jnp.zeros((nb, bl), jnp.int32)
    for slot in range(DOC_DEV):
        n = jnp.sum(jnp.where(doc == slot, livef, 0.0), axis=1, keepdims=True)
        more = jnp.maximum(chunks(n.astype(jnp.int32) - 1), 0)
        before = before + jnp.where(doc > slot, n, 0.0)
        extra = extra + jnp.where(doc > slot, more, 0)
    rank = (counted - livef - before).astype(jnp.int32)
    part = chunks(rank)
    group = rank - part * CHUNK
    row = group * 8 + jnp.where(part == 0, doc, ROWS // 2 + extra + part - 1)
    return jnp.where(live, row, -1), jnp.where(live, doc, -1)


def pack_blocks(project, groups, w_ref, row_ref, doc_ref, start, out_ref, meta_ref):
    bl = row_ref.shape[1]
    dim = w_ref.shape[1]
    sub = lax.broadcasted_iota(jnp.int32, (8, bl), 0)
    earlier = (
        lax.broadcasted_iota(jnp.int32, (8, 8), 0) > lax.broadcasted_iota(jnp.int32, (8, 8), 1)
    ).astype(jnp.float32)
    coming = project(0)
    for g in range(groups):
        vectors = coming
        if g + 1 < groups:
            coming = project(g + 1)
        for u in range(GROUP):
            b = g * GROUP + u
            row = row_ref[start + b : start + b + 1, :]
            tiles = []
            for tile in range(2):
                hits = [
                    (row == sub + (ROWS // 2 * tile + 8 * i)).astype(jnp.float32)
                    for i in range(CHUNK)
                ]
                count = jnp.sum(functools.reduce(jnp.add, hits), axis=1, keepdims=True)
                tiles += hits[:1]
                tiles += [jnp.where(count > float(i), hits[i], hits[0]) for i in range(1, CHUNK)]
            pick = jnp.concatenate(tiles, axis=0).astype(jnp.bfloat16)
            out_ref[b] = jnp.dot(
                pick, vectors[u * bl : (u + 1) * bl], preferred_element_type=jnp.float32
            ).astype(jnp.bfloat16)
            doc = doc_ref[start + b : start + b + 1, :]
            n = jnp.sum((doc == sub).astype(jnp.float32), axis=1, keepdims=True)
            n = jnp.broadcast_to(n, (8, dim)).astype(jnp.int32)
            more = jnp.maximum(chunks(n - 1), 0)
            first = jnp.dot(
                earlier, more.astype(jnp.float32), preferred_element_type=jnp.float32
            ).astype(jnp.int32)
            meta_ref[b, 0] = n
            meta_ref[b, 1] = more
            for j in range(FURTHER):
                meta_ref[b, 2 + j] = jnp.maximum(jnp.minimum(more - 1, j), 0) + jnp.minimum(first, 7)


def vectors_of(h, w):
    projected = jnp.dot(h.reshape(-1, h.shape[-1]), w, preferred_element_type=jnp.float32)
    total = jnp.sum(projected * projected, axis=1, keepdims=True)
    return (projected * lax.rsqrt(total + 1e-06)).astype(jnp.bfloat16)


def pack_first_kernel(
    h_hbm, w_hbm, doc_hbm, live_hbm, out_ref, meta_ref, next_ref, w_ref, row_ref, doc_ref, *scratch
):
    h_ref, token_ref, live_ref, sems = scratch
    nb, count = h_ref.shape[0], next_ref.shape[0]
    groups = nb // GROUP
    small = [
        pltpu.make_async_copy(doc_hbm, token_ref, sems.at[0]),
        pltpu.make_async_copy(live_hbm, live_ref, sems.at[1]),
        pltpu.make_async_copy(w_hbm, w_ref, sems.at[2]),
    ]
    large = [
        pltpu.make_async_copy(
            h_hbm.at[pl.ds(g * GROUP, GROUP)], h_ref.at[pl.ds(g * GROUP, GROUP)], sems.at[4 + g]
        )
        for g in range(groups)
    ]
    later = pltpu.make_async_copy(h_hbm.at[pl.ds(nb, count)], next_ref, sems.at[3])
    for copy in small + large + [later]:
        copy.start()
    small[0].wait()
    small[1].wait()
    row, doc = place_tokens(token_ref[...], live_ref[...] == 1)
    row_ref[...] = row
    doc_ref[...] = doc
    small[2].wait()
    for copy in large:
        copy.wait()

    def project(g):
        return vectors_of(h_ref[g * GROUP : (g + 1) * GROUP], w_ref[...])

    once(lambda: pack_blocks(project, groups, w_ref, row_ref, doc_ref, 0, out_ref, meta_ref))
    later.wait()


def pack_next_kernel(h_ref, w_ref, row_ref, doc_ref, *refs, start, more):
    nb = h_ref.shape[0]
    if more:
        h_hbm, out_ref, meta_ref, next_ref, sem = refs
        later = pltpu.make_async_copy(
            h_hbm.at[pl.ds(start + nb, next_ref.shape[0])], next_ref, sem.at[0]
        )
        later.start()
    else:
        out_ref, meta_ref = refs

    def project(g):
        return vectors_of(h_ref[g * GROUP : (g + 1) * GROUP], w_ref[...])

    groups = nb // GROUP
    once(lambda: pack_blocks(project, groups, w_ref, row_ref, doc_ref, start, out_ref, meta_ref))
    if more:
        later.wait()


def pack(hidden_states, proj_weight, token_doc, token_live):
    nblocks, bl, d = hidden_states.shape
    dim = proj_weight.shape[1]
    sizes = [nblocks * share // sum(PARTS) for share in PARTS]
    starts = [sum(sizes[:i]) for i in range(len(sizes))]
    hidden = in_hbm(hidden_states)

    def outputs(i):
        shapes = [
            pltpu.VMEM((sizes[i], ROWS, dim), jnp.bfloat16),
            pltpu.VMEM((sizes[i], 2 + FURTHER, 8, dim), jnp.int32),
        ]
        if i + 1 < len(sizes):
            shapes.append(pltpu.VMEM((sizes[i + 1], bl, d), hidden_states.dtype))
        return shapes

    def cost(i):
        tokens = sizes[i] * bl
        return pl.CostEstimate(
            flops=2 * tokens * d * dim, bytes_accessed=2 * tokens * d, transcendentals=tokens
        )

    def first():
        shapes = outputs(0) + [
            pltpu.VMEM((d, dim), proj_weight.dtype),
            pltpu.VMEM((nblocks, bl), jnp.int32),
            pltpu.VMEM((nblocks, bl), jnp.int32),
        ]
        return pl.pallas_call(
            pack_first_kernel,
            in_specs=[pl.BlockSpec(memory_space=pltpu.HBM)] * 4,
            out_specs=[VMEM] * len(shapes),
            out_shape=shapes,
            scratch_shapes=[
                pltpu.VMEM((sizes[0], bl, d), hidden_states.dtype),
                pltpu.VMEM((nblocks, bl), jnp.int32),
                pltpu.VMEM((nblocks, bl), jnp.int32),
                pltpu.SemaphoreType.DMA((4 + sizes[0] // GROUP,)),
            ],
            cost_estimate=cost(0),
            compiler_params=PARAMS,
            name="pack_first",
        )(hidden, *(in_hbm(x) for x in (proj_weight, token_doc, token_live)))

    def following(i, fetched, weight, row, doc):
        more = i + 1 < len(sizes)
        return pl.pallas_call(
            functools.partial(pack_next_kernel, start=starts[i], more=more),
            in_specs=[VMEM] * 4 + [pl.BlockSpec(memory_space=pltpu.HBM)] * more,
            out_specs=[VMEM] * (3 if more else 2),
            out_shape=outputs(i),
            scratch_shapes=[pltpu.SemaphoreType.DMA((1,))] * more,
            cost_estimate=cost(i),
            compiler_params=PARAMS,
            name="pack_next",
        )(fetched, weight, row, doc, *[hidden] * more)

    packed, meta = [], []
    for i in range(len(sizes)):
        if i == 0:
            vectors, layout, *left, weight, row, doc = first()
        else:
            vectors, layout, *left = following(i, left[0], weight, row, doc)
        packed.append(vectors)
        meta.append(layout)
    return packed, meta


def score_kernel(owner_ref, *refs, parts, pieces, width):
    vec_refs, meta_refs = refs[:parts], refs[parts : 2 * parts]
    got_refs = refs[2 * parts : 2 * parts + pieces]
    keep_ref, send_ref, unit_ref, query_ref, table_ref = refs[2 * parts + pieces :]
    n = lax.axis_size("wide")
    bits = n.bit_length() - 1
    me = lax.axis_index("wide")
    columns = query_ref.shape[0]
    piece = columns // (n // 2)
    largest = jnp.zeros((16, query_ref.shape[1]), jnp.float32)
    j = 0
    for got_ref in got_refs:
        for k in range(got_ref.shape[0] // piece):
            chip = (me >> 1) ^ bit_reverse(j, bits - 1)
            block = got_ref[k * piece : (k + 1) * piece, :]
            query_ref[pl.ds(pl.multiple_of(chip * piece, piece), piece), :] = block
            size = jnp.abs(block.astype(jnp.float32))
            for r in range(0, piece, 16):
                largest = jnp.maximum(largest, size[r : r + 16])
            j += 1
    unit = jnp.max(jnp.max(largest, axis=1, keepdims=True), axis=0, keepdims=True)
    unit = jnp.broadcast_to(jnp.where(unit > 0.0, unit, 1.0) * (1.0 / SCALE), unit_ref.shape)
    unit_ref[...] = unit
    table_ref[...] = jnp.full(table_ref.shape, LOW, jnp.float32)
    span = min(columns, 512)

    def visit(vec_ref, meta_ref, b, offset, start):
        rows = pl.ds(pl.multiple_of(owner_ref[offset + b] * DOC_DEV, DOC_DEV), DOC_DEV)
        some = [meta_ref[b, tile] > 0 for tile in range(2)]
        index = [meta_ref[b, 2 + j] for j in range(FURTHER)]
        tokens = vec_ref[b]
        for t in range(span // width):
            at = pl.ds(start + t * width, width)
            similar = lax.dot_general(
                tokens,
                query_ref[at, :],
                (((1,), (1,)), ((), ())),
                preferred_element_type=jnp.float32,
            )
            first, rest = (
                functools.reduce(
                    jnp.maximum,
                    [similar[base + 8 * g : base + 8 * g + 8] for g in range(CHUNK)],
                )
                for base in (0, ROWS // 2)
            )
            best = []
            for c in range(width // 128):
                lanes = slice(c * 128, (c + 1) * 128)
                further = functools.reduce(
                    jnp.maximum,
                    [jnp.take_along_axis(rest[:, lanes], at8, axis=0) for at8 in index],
                )
                top = jnp.where(some[0], first[:, lanes], LOW)
                top = jnp.maximum(top, jnp.where(some[1], further, LOW))
                best.append(top)
            table_ref[rows, at] = jnp.maximum(table_ref[rows, at], jnp.concatenate(best, axis=1))

    def over_blocks(start):
        offset = 0
        for vec_ref, meta_ref in zip(vec_refs, meta_refs):
            nb = vec_ref.shape[0]
            step = next(s for s in (UNROLL, 24, 16, 8, 4, 2, 1) if nb % s == 0)

            def some_blocks(i, carry, vec_ref=vec_ref, meta_ref=meta_ref, offset=offset, step=step):
                for u in range(step):
                    visit(vec_ref, meta_ref, i * step + u, offset, start)
                return carry

            lax.fori_loop(0, nb // step, some_blocks, 0)
            offset += nb

    if columns == span:
        over_blocks(0)
    else:

        def one_span(i, carry):
            over_blocks(pl.multiple_of(i * span, span))
            return carry

        lax.fori_loop(0, columns // span, one_span, 0)
    factor = 1.0 / unit[:1, :1]
    for place in range(n):
        high = bit_reverse(place % (n // 2), bits - 1)
        owner = me ^ (high << 1 | (place // (n // 2) ^ parity(high, bits)))
        rows = table_ref[pl.ds(pl.multiple_of(owner * DOC_DEV, DOC_DEV), DOC_DEV), :]
        out_ref = send_ref if place >= n // 2 else keep_ref
        start = place % (n // 2) * DOC_DEV
        out_ref[start : start + DOC_DEV, :] = jnp.maximum(rows * factor, NONE)


def score(owner, packed, meta, gathered, owners):
    dim = gathered[0].shape[1]
    columns = sum(piece.shape[0] for piece in gathered)
    rows = sum(p.shape[0] * p.shape[1] for p in packed)
    half = (owners * DOC_DEV // 2, columns)
    return pl.pallas_call(
        functools.partial(score_kernel, parts=len(packed), pieces=len(gathered), width=256),
        in_specs=[pl.BlockSpec(memory_space=pltpu.SMEM)] + [VMEM] * (2 * len(packed) + len(gathered)),
        out_specs=[VMEM] * 3,
        out_shape=[
            pltpu.VMEM(half, jnp.float32),
            pltpu.VMEM(half, jnp.float32),
            pltpu.VMEM((8, 128), jnp.float32),
        ],
        scratch_shapes=[
            pltpu.VMEM((columns, dim), jnp.bfloat16),
            pltpu.VMEM((owners * DOC_DEV, columns), jnp.float32),
        ],
        cost_estimate=pl.CostEstimate(
            flops=2 * rows * dim * columns, bytes_accessed=4 * rows * dim, transcendentals=0
        ),
        compiler_params=PARAMS,
    )(owner, *packed, *meta, *(in_vmem(x) for x in gathered))


def in_hbm(x):
    return pltpu.with_memory_space_constraint(x, pltpu.HBM)


def in_vmem(x):
    return pltpu.with_memory_space_constraint(x, pltpu.VMEM)


def finish_kernel(keep_ref, got_ref, unit_a_ref, unit_b_ref, out_ref):
    best = jnp.maximum(keep_ref[...], got_ref[...])
    half = best.shape[1] // 2
    best = jnp.where(best > 0.9 * NONE, best, 0.0)
    best = jnp.concatenate(
        [best[:, :half] * unit_a_ref[:1, :1], best[:, half:] * unit_b_ref[:1, :1]], axis=1
    )
    bits = lax.axis_size("wide").bit_length() - 1
    odd = parity(lax.axis_index("wide"), bits) == 1
    even_queries = jnp.where(odd, best[:, half:], best[:, :half])
    odd_queries = jnp.where(odd, best[:, :half], best[:, half:])
    low = lax.broadcasted_iota(jnp.int32, (best.shape[0], 128), 1) < 64
    for chip in range(half // 64):
        at = slice(chip // 2 * 128, chip // 2 * 128 + 128)
        a, b = even_queries[:, at], odd_queries[:, at]
        if parity(chip, bits):
            a, b = b, a
        if chip % 2:
            a = pltpu.roll(a, 64, 1)
        else:
            b = pltpu.roll(b, 64, 1)
        out_ref[:, chip * 128 : (chip + 1) * 128] = jnp.where(low, a, b)


def finish(keep, got, unit_a, unit_b):
    return pl.pallas_call(
        finish_kernel,
        in_specs=[VMEM] * 4,
        out_specs=VMEM,
        out_shape=jax.ShapeDtypeStruct(keep.shape, jnp.float32),
        compiler_params=PARAMS,
        name="finish",
    )(*(in_vmem(x) for x in (keep, got, unit_a, unit_b)))


def program(hidden_states, block_owner, token_doc, token_live, proj_weight, queries):
    n = lax.axis_size("wide")
    if n & (n - 1) or queries.shape[0] != 64:
        raise ValueError("sizes")

    def swap(x, stride):
        return lax.ppermute(x, "wide", [(i, i ^ stride) for i in range(n)])

    strides = [1] + [(1 << bit) | 1 for bit in range(1, n.bit_length() - 1)]
    packed, meta = pack(hidden_states, proj_weight, token_doc, token_live)
    pieces, mine = [queries], queries
    for stride in reversed(strides[1:]):
        pieces.append(swap(mine, stride))
        mine = lax.optimization_barrier(jnp.concatenate([mine, pieces[-1]], axis=0))
    other = swap(mine, 1)
    owner = block_owner.reshape(-1)
    keep_a, send_a, unit_a = score(owner, packed, meta, pieces, n)
    got_b = swap(send_a.astype(SENT), 1)
    keep_b, send_b, unit_b = score(owner, packed, meta, [other], n)
    got_a = swap(send_b.astype(SENT), 1)
    best = jnp.concatenate(
        [
            jnp.maximum(keep_a, got_a.astype(jnp.float32)),
            jnp.maximum(keep_b, got_b.astype(jnp.float32)),
        ],
        axis=1,
    )
    for stride in strides[1:]:
        half = best.shape[0] // 2
        keep, got = best[:half], swap(best[half:].astype(SENT), stride)
        if stride != strides[-1]:
            best = jnp.maximum(keep, got.astype(jnp.float32))
    return finish(keep, got.astype(jnp.float32), unit_a, unit_b)


def solution(mesh):
    placed = (
        P(("groups", "wide"), None, None),
        P(("groups", "wide"), None),
        P(("groups", "wide"), None),
        P(("groups", "wide"), None),
        P(),
        P(("groups", "wide"), None),
    )
    return jax.shard_map(
        program, mesh=mesh, in_specs=placed, out_specs=P(("groups", "wide"), None), check_vma=False
    )
```

```python
import functools

import jax
import jax.numpy as jnp
from jax import lax
from jax.experimental import pallas as pl
from jax.experimental.pallas import tpu as pltpu
from jax.sharding import PartitionSpec as P


DOC_DEV = 8
CHUNK = 7
TOGETHER = 8
ROWS = 2 * CHUNK * DOC_DEV
FURTHER = 4
GROUP = 8
UNROLL = 32
LOW = -1000000000.0
SENT = jnp.float16
SCALE = 4096.0
NONE = -60000.0
PARTS = (1, 3, 4)

VMEM = pl.BlockSpec(memory_space=pltpu.VMEM)
PARAMS = pltpu.CompilerParams(vmem_limit_bytes=24 << 20)


def bit_reverse(value, bits):
    out = value * 0
    for bit in range(bits):
        out = out | (((value >> bit) & 1) << (bits - 1 - bit))
    return out


def parity(value, bits):
    out = value * 0
    for bit in range(bits):
        out = out ^ ((value >> bit) & 1)
    return out


def chunks(value):
    return (value * 37) >> 8


def once(body):
    def run(i, carry):
        body()
        return carry

    lax.fori_loop(0, 1 + (lax.axis_index("wide") >> 20), run, 0)


def place_tokens(doc, live):
    nb, bl = doc.shape
    livef = live.astype(jnp.float32)
    upto = lax.broadcasted_iota(jnp.int32, (bl, bl), 0) <= lax.broadcasted_iota(
        jnp.int32, (bl, bl), 1
    )
    counted = jnp.dot(livef, upto.astype(jnp.float32), preferred_element_type=jnp.float32)
    before = jnp.zeros((nb, bl), jnp.float32)
    extra = jnp.zeros((nb, bl), jnp.int32)
    for slot in range(DOC_DEV):
        n = jnp.sum(jnp.where(doc == slot, livef, 0.0), axis=1, keepdims=True)
        more = jnp.maximum(chunks(n.astype(jnp.int32) - 1), 0)
        before = before + jnp.where(doc > slot, n, 0.0)
        extra = extra + jnp.where(doc > slot, more, 0)
    rank = (counted - livef - before).astype(jnp.int32)
    part = chunks(rank)
    group = rank - part * CHUNK
    row = group * 8 + jnp.where(part == 0, doc, ROWS // 2 + extra + part - 1)
    return jnp.where(live, row, -1), jnp.where(live, doc, -1)


def pack_blocks(project, groups, w_ref, row_ref, doc_ref, start, out_ref, meta_ref):
    bl = row_ref.shape[1]
    dim = w_ref.shape[1]
    sub = lax.broadcasted_iota(jnp.int32, (8, bl), 0)
    earlier = (
        lax.broadcasted_iota(jnp.int32, (8, 8), 0) > lax.broadcasted_iota(jnp.int32, (8, 8), 1)
    ).astype(jnp.float32)
    coming = project(0)
    for g in range(groups):
        vectors = coming
        if g + 1 < groups:
            coming = project(g + 1)
        for u in range(GROUP):
            b = g * GROUP + u
            row = row_ref[start + b : start + b + 1, :]
            tiles = []
            for tile in range(2):
                hits = [
                    (row == sub + (ROWS // 2 * tile + 8 * i)).astype(jnp.float32)
                    for i in range(CHUNK)
                ]
                count = jnp.sum(functools.reduce(jnp.add, hits), axis=1, keepdims=True)
                tiles += hits[:1]
                tiles += [jnp.where(count > float(i), hits[i], hits[0]) for i in range(1, CHUNK)]
            pick = jnp.concatenate(tiles, axis=0).astype(jnp.bfloat16)
            out_ref[b] = jnp.dot(
                pick, vectors[u * bl : (u + 1) * bl], preferred_element_type=jnp.float32
            ).astype(jnp.bfloat16)
            doc = doc_ref[start + b : start + b + 1, :]
            n = jnp.sum((doc == sub).astype(jnp.float32), axis=1, keepdims=True)
            n = jnp.broadcast_to(n, (8, dim)).astype(jnp.int32)
            more = jnp.maximum(chunks(n - 1), 0)
            first = jnp.dot(
                earlier, more.astype(jnp.float32), preferred_element_type=jnp.float32
            ).astype(jnp.int32)
            meta_ref[b, 0] = n
            meta_ref[b, 1] = more
            for j in range(FURTHER):
                meta_ref[b, 2 + j] = jnp.maximum(jnp.minimum(more - 1, j), 0) + jnp.minimum(first, 7)


def vectors_of(h, w):
    projected = jnp.dot(h.reshape(-1, h.shape[-1]), w, preferred_element_type=jnp.float32)
    total = jnp.sum(projected * projected, axis=1, keepdims=True)
    return (projected * lax.rsqrt(total + 1e-06)).astype(jnp.bfloat16)


def pack_first_kernel(
    h_hbm, w_hbm, doc_hbm, live_hbm, out_ref, meta_ref, next_ref, w_ref, row_ref, doc_ref, *scratch
):
    h_ref, token_ref, live_ref, sems = scratch
    nb, count = h_ref.shape[0], next_ref.shape[0]
    groups = nb // GROUP
    small = [
        pltpu.make_async_copy(doc_hbm, token_ref, sems.at[0]),
        pltpu.make_async_copy(live_hbm, live_ref, sems.at[1]),
        pltpu.make_async_copy(w_hbm, w_ref, sems.at[2]),
    ]
    large = [
        pltpu.make_async_copy(
            h_hbm.at[pl.ds(g * GROUP, GROUP)], h_ref.at[pl.ds(g * GROUP, GROUP)], sems.at[4 + g]
        )
        for g in range(groups)
    ]
    later = pltpu.make_async_copy(h_hbm.at[pl.ds(nb, count)], next_ref, sems.at[3])
    for copy in small + large + [later]:
        copy.start()
    small[0].wait()
    small[1].wait()
    row, doc = place_tokens(token_ref[...], live_ref[...] == 1)
    row_ref[...] = row
    doc_ref[...] = doc
    small[2].wait()
    for copy in large:
        copy.wait()

    def project(g):
        return vectors_of(h_ref[g * GROUP : (g + 1) * GROUP], w_ref[...])

    once(lambda: pack_blocks(project, groups, w_ref, row_ref, doc_ref, 0, out_ref, meta_ref))
    later.wait()


def pack_next_kernel(h_ref, w_ref, row_ref, doc_ref, *refs, start, more):
    nb = h_ref.shape[0]
    if more:
        h_hbm, out_ref, meta_ref, next_ref, sem = refs
        later = pltpu.make_async_copy(
            h_hbm.at[pl.ds(start + nb, next_ref.shape[0])], next_ref, sem.at[0]
        )
        later.start()
    else:
        out_ref, meta_ref = refs

    def project(g):
        return vectors_of(h_ref[g * GROUP : (g + 1) * GROUP], w_ref[...])

    groups = nb // GROUP
    once(lambda: pack_blocks(project, groups, w_ref, row_ref, doc_ref, start, out_ref, meta_ref))
    if more:
        later.wait()


def pack(hidden_states, proj_weight, token_doc, token_live):
    nblocks, bl, d = hidden_states.shape
    dim = proj_weight.shape[1]
    sizes = [nblocks * share // sum(PARTS) for share in PARTS]
    starts = [sum(sizes[:i]) for i in range(len(sizes))]
    hidden = in_hbm(hidden_states)

    def outputs(i):
        shapes = [
            pltpu.VMEM((sizes[i], ROWS, dim), jnp.bfloat16),
            pltpu.VMEM((sizes[i], 2 + FURTHER, 8, dim), jnp.int32),
        ]
        if i + 1 < len(sizes):
            shapes.append(pltpu.VMEM((sizes[i + 1], bl, d), hidden_states.dtype))
        return shapes

    def cost(i):
        tokens = sizes[i] * bl
        return pl.CostEstimate(
            flops=2 * tokens * d * dim, bytes_accessed=2 * tokens * d, transcendentals=tokens
        )

    def first():
        shapes = outputs(0) + [
            pltpu.VMEM((d, dim), proj_weight.dtype),
            pltpu.VMEM((nblocks, bl), jnp.int32),
            pltpu.VMEM((nblocks, bl), jnp.int32),
        ]
        return pl.pallas_call(
            pack_first_kernel,
            in_specs=[pl.BlockSpec(memory_space=pltpu.HBM)] * 4,
            out_specs=[VMEM] * len(shapes),
            out_shape=shapes,
            scratch_shapes=[
                pltpu.VMEM((sizes[0], bl, d), hidden_states.dtype),
                pltpu.VMEM((nblocks, bl), jnp.int32),
                pltpu.VMEM((nblocks, bl), jnp.int32),
                pltpu.SemaphoreType.DMA((4 + sizes[0] // GROUP,)),
            ],
            cost_estimate=cost(0),
            compiler_params=PARAMS,
            name="pack_first",
        )(hidden, *(in_hbm(x) for x in (proj_weight, token_doc, token_live)))

    def following(i, fetched, weight, row, doc):
        more = i + 1 < len(sizes)
        return pl.pallas_call(
            functools.partial(pack_next_kernel, start=starts[i], more=more),
            in_specs=[VMEM] * 4 + [pl.BlockSpec(memory_space=pltpu.HBM)] * more,
            out_specs=[VMEM] * (3 if more else 2),
            out_shape=outputs(i),
            scratch_shapes=[pltpu.SemaphoreType.DMA((1,))] * more,
            cost_estimate=cost(i),
            compiler_params=PARAMS,
            name="pack_next",
        )(fetched, weight, row, doc, *[hidden] * more)

    packed, meta = [], []
    for i in range(len(sizes)):
        if i == 0:
            vectors, layout, *left, weight, row, doc = first()
        else:
            vectors, layout, *left = following(i, left[0], weight, row, doc)
        packed.append(vectors)
        meta.append(layout)
    return packed, meta


def score_kernel(owner_ref, *refs, parts, pieces, width):
    vec_refs, meta_refs = refs[:parts], refs[parts : 2 * parts]
    got_refs = refs[2 * parts : 2 * parts + pieces]
    keep_ref, send_ref, unit_ref, query_ref, table_ref = refs[2 * parts + pieces :]
    n = lax.axis_size("wide")
    bits = n.bit_length() - 1
    me = lax.axis_index("wide")
    columns = query_ref.shape[0]
    piece = columns // (n // 2)
    largest = jnp.zeros((16, query_ref.shape[1]), jnp.float32)
    j = 0
    for got_ref in got_refs:
        for k in range(got_ref.shape[0] // piece):
            chip = (me >> 1) ^ bit_reverse(j, bits - 1)
            block = got_ref[k * piece : (k + 1) * piece, :]
            query_ref[pl.ds(pl.multiple_of(chip * piece, piece), piece), :] = block
            size = jnp.abs(block.astype(jnp.float32))
            for r in range(0, piece, 16):
                largest = jnp.maximum(largest, size[r : r + 16])
            j += 1
    unit = jnp.max(jnp.max(largest, axis=1, keepdims=True), axis=0, keepdims=True)
    unit = jnp.broadcast_to(jnp.where(unit > 0.0, unit, 1.0) * (1.0 / SCALE), unit_ref.shape)
    unit_ref[...] = unit
    table_ref[...] = jnp.full(table_ref.shape, LOW, jnp.float32)
    span = min(columns, 512)

    def visit(vec_ref, meta_ref, b, offset, start):
        tokens = vec_ref[pl.ds(b, TOGETHER)].reshape(TOGETHER * ROWS, -1)
        for t in range(span // width):
            at = pl.ds(start + t * width, width)
            similar = lax.dot_general(
                tokens,
                query_ref[at, :],
                (((1,), (1,)), ((), ())),
                preferred_element_type=jnp.float32,
            )
            for u in range(TOGETHER):
                merge(similar[u * ROWS : (u + 1) * ROWS], meta_ref, b + u, offset, at)

    def merge(similar, meta_ref, b, offset, at):
        rows = pl.ds(pl.multiple_of(owner_ref[offset + b] * DOC_DEV, DOC_DEV), DOC_DEV)
        some = [meta_ref[b, tile] > 0 for tile in range(2)]
        index = [meta_ref[b, 2 + j] for j in range(FURTHER)]
        first, rest = (
            functools.reduce(
                jnp.maximum,
                [similar[base + 8 * g : base + 8 * g + 8] for g in range(CHUNK)],
            )
            for base in (0, ROWS // 2)
        )
        best = []
        for c in range(width // 128):
            lanes = slice(c * 128, (c + 1) * 128)
            further = functools.reduce(
                jnp.maximum, [jnp.take_along_axis(rest[:, lanes], at8, axis=0) for at8 in index]
            )
            top = jnp.where(some[0], first[:, lanes], LOW)
            best.append(jnp.maximum(top, jnp.where(some[1], further, LOW)))
        table_ref[rows, at] = jnp.maximum(table_ref[rows, at], jnp.concatenate(best, axis=1))

    def over_blocks(start):
        offset = 0
        for vec_ref, meta_ref in zip(vec_refs, meta_refs):
            nb = vec_ref.shape[0]
            step = next(s for s in (UNROLL, 24, 16, 8) if nb % s == 0)

            def some_blocks(i, carry, vec_ref=vec_ref, meta_ref=meta_ref, offset=offset, step=step):
                for u in range(0, step, TOGETHER):
                    visit(vec_ref, meta_ref, i * step + u, offset, start)
                return carry

            lax.fori_loop(0, nb // step, some_blocks, 0)
            offset += nb

    if columns == span:
        over_blocks(0)
    else:

        def one_span(i, carry):
            over_blocks(pl.multiple_of(i * span, span))
            return carry

        lax.fori_loop(0, columns // span, one_span, 0)
    factor = 1.0 / unit[:1, :1]
    for place in range(n):
        high = bit_reverse(place % (n // 2), bits - 1)
        owner = me ^ (high << 1 | (place // (n // 2) ^ parity(high, bits)))
        rows = table_ref[pl.ds(pl.multiple_of(owner * DOC_DEV, DOC_DEV), DOC_DEV), :]
        out_ref = send_ref if place >= n // 2 else keep_ref
        start = place % (n // 2) * DOC_DEV
        out_ref[start : start + DOC_DEV, :] = jnp.maximum(rows * factor, NONE)


def score(owner, packed, meta, gathered, owners):
    dim = gathered[0].shape[1]
    columns = sum(piece.shape[0] for piece in gathered)
    rows = sum(p.shape[0] * p.shape[1] for p in packed)
    half = (owners * DOC_DEV // 2, columns)
    return pl.pallas_call(
        functools.partial(score_kernel, parts=len(packed), pieces=len(gathered), width=256),
        in_specs=[pl.BlockSpec(memory_space=pltpu.SMEM)] + [VMEM] * (2 * len(packed) + len(gathered)),
        out_specs=[VMEM] * 3,
        out_shape=[
            pltpu.VMEM(half, jnp.float32),
            pltpu.VMEM(half, jnp.float32),
            pltpu.VMEM((8, 128), jnp.float32),
        ],
        scratch_shapes=[
            pltpu.VMEM((columns, dim), jnp.bfloat16),
            pltpu.VMEM((owners * DOC_DEV, columns), jnp.float32),
        ],
        cost_estimate=pl.CostEstimate(
            flops=2 * rows * dim * columns, bytes_accessed=4 * rows * dim, transcendentals=0
        ),
        compiler_params=PARAMS,
    )(owner, *packed, *meta, *(in_vmem(x) for x in gathered))


def in_hbm(x):
    return pltpu.with_memory_space_constraint(x, pltpu.HBM)


def in_vmem(x):
    return pltpu.with_memory_space_constraint(x, pltpu.VMEM)


def finish_kernel(keep_ref, got_ref, unit_a_ref, unit_b_ref, out_ref):
    best = jnp.maximum(keep_ref[...], got_ref[...])
    half = best.shape[1] // 2
    best = jnp.where(best > 0.9 * NONE, best, 0.0)
    best = jnp.concatenate(
        [best[:, :half] * unit_a_ref[:1, :1], best[:, half:] * unit_b_ref[:1, :1]], axis=1
    )
    bits = lax.axis_size("wide").bit_length() - 1
    odd = parity(lax.axis_index("wide"), bits) == 1
    even_queries = jnp.where(odd, best[:, half:], best[:, :half])
    odd_queries = jnp.where(odd, best[:, :half], best[:, half:])
    low = lax.broadcasted_iota(jnp.int32, (best.shape[0], 128), 1) < 64
    for chip in range(half // 64):
        at = slice(chip // 2 * 128, chip // 2 * 128 + 128)
        a, b = even_queries[:, at], odd_queries[:, at]
        if parity(chip, bits):
            a, b = b, a
        if chip % 2:
            a = pltpu.roll(a, 64, 1)
        else:
            b = pltpu.roll(b, 64, 1)
        out_ref[:, chip * 128 : (chip + 1) * 128] = jnp.where(low, a, b)


def finish(keep, got, unit_a, unit_b):
    return pl.pallas_call(
        finish_kernel,
        in_specs=[VMEM] * 4,
        out_specs=VMEM,
        out_shape=jax.ShapeDtypeStruct(keep.shape, jnp.float32),
        compiler_params=PARAMS,
        name="finish",
    )(*(in_vmem(x) for x in (keep, got, unit_a, unit_b)))


def program(hidden_states, block_owner, token_doc, token_live, proj_weight, queries):
    n = lax.axis_size("wide")
    if n & (n - 1) or queries.shape[0] != 64:
        raise ValueError("sizes")

    def swap(x, stride):
        return lax.ppermute(x, "wide", [(i, i ^ stride) for i in range(n)])

    strides = [1] + [(1 << bit) | 1 for bit in range(1, n.bit_length() - 1)]
    packed, meta = pack(hidden_states, proj_weight, token_doc, token_live)
    pieces, mine = [queries], queries
    for stride in reversed(strides[1:]):
        pieces.append(swap(mine, stride))
        mine = lax.optimization_barrier(jnp.concatenate([mine, pieces[-1]], axis=0))
    other = swap(mine, 1)
    owner = block_owner.reshape(-1)
    keep_a, send_a, unit_a = score(owner, packed, meta, pieces, n)
    got_b = swap(send_a.astype(SENT), 1)
    keep_b, send_b, unit_b = score(owner, packed, meta, [other], n)
    got_a = swap(send_b.astype(SENT), 1)
    best = jnp.concatenate(
        [
            jnp.maximum(keep_a, got_a.astype(jnp.float32)),
            jnp.maximum(keep_b, got_b.astype(jnp.float32)),
        ],
        axis=1,
    )
    for stride in strides[1:]:
        half = best.shape[0] // 2
        keep, got = best[:half], swap(best[half:].astype(SENT), stride)
        if stride != strides[-1]:
            best = jnp.maximum(keep, got.astype(jnp.float32))
    return finish(keep, got.astype(jnp.float32), unit_a, unit_b)


def solution(mesh):
    placed = (
        P(("groups", "wide"), None, None),
        P(("groups", "wide"), None),
        P(("groups", "wide"), None),
        P(("groups", "wide"), None),
        P(),
        P(("groups", "wide"), None),
    )
    return jax.shard_map(
        program, mesh=mesh, in_specs=placed, out_specs=P(("groups", "wide"), None), check_vma=False
    )
```

```python
import functools

import jax
import jax.numpy as jnp
from jax import lax
from jax.experimental import pallas as pl
from jax.experimental.pallas import tpu as pltpu
from jax.sharding import PartitionSpec as P


DOC_DEV = 8
CHUNK = 7
TOGETHER = 8
ROWS = 2 * CHUNK * DOC_DEV
FURTHER = 4
GROUP = 8
UNROLL = 32
LOW = -1000000000.0
SENT = jnp.float16
SCALE = 4096.0
NONE = -60000.0
PARTS = (1, 3, 4)

VMEM = pl.BlockSpec(memory_space=pltpu.VMEM)
PARAMS = pltpu.CompilerParams(vmem_limit_bytes=24 << 20)


def bit_reverse(value, bits):
    out = value * 0
    for bit in range(bits):
        out = out | (((value >> bit) & 1) << (bits - 1 - bit))
    return out


def parity(value, bits):
    out = value * 0
    for bit in range(bits):
        out = out ^ ((value >> bit) & 1)
    return out


def chunks(value):
    return (value * 37) >> 8


def once(body):
    def run(i, carry):
        body()
        return carry

    lax.fori_loop(0, 1 + (lax.axis_index("wide") >> 20), run, 0)


def place_tokens(doc, live):
    nb, bl = doc.shape
    livef = live.astype(jnp.float32)
    upto = lax.broadcasted_iota(jnp.int32, (bl, bl), 0) <= lax.broadcasted_iota(
        jnp.int32, (bl, bl), 1
    )
    counted = jnp.dot(livef, upto.astype(jnp.float32), preferred_element_type=jnp.float32)
    before = jnp.zeros((nb, bl), jnp.float32)
    extra = jnp.zeros((nb, bl), jnp.int32)
    for slot in range(DOC_DEV):
        n = jnp.sum(jnp.where(doc == slot, livef, 0.0), axis=1, keepdims=True)
        more = jnp.maximum(chunks(n.astype(jnp.int32) - 1), 0)
        before = before + jnp.where(doc > slot, n, 0.0)
        extra = extra + jnp.where(doc > slot, more, 0)
    rank = (counted - livef - before).astype(jnp.int32)
    part = chunks(rank)
    group = rank - part * CHUNK
    row = group * 8 + jnp.where(part == 0, doc, ROWS // 2 + extra + part - 1)
    return jnp.where(live, row, -1), jnp.where(live, doc, -1)


def pack_blocks(project, groups, w_ref, row_ref, doc_ref, start, out_ref, meta_ref):
    bl = row_ref.shape[1]
    dim = w_ref.shape[1]
    sub = lax.broadcasted_iota(jnp.int32, (8, bl), 0)
    earlier = (
        lax.broadcasted_iota(jnp.int32, (8, 8), 0) > lax.broadcasted_iota(jnp.int32, (8, 8), 1)
    ).astype(jnp.float32)
    coming = project(0)
    for g in range(groups):
        vectors = coming
        if g + 1 < groups:
            coming = project(g + 1)
        for u in range(GROUP):
            b = g * GROUP + u
            row = row_ref[start + b : start + b + 1, :]
            tiles = []
            for tile in range(2):
                hits = [
                    (row == sub + (ROWS // 2 * tile + 8 * i)).astype(jnp.float32)
                    for i in range(CHUNK)
                ]
                count = jnp.sum(functools.reduce(jnp.add, hits), axis=1, keepdims=True)
                tiles += hits[:1]
                tiles += [jnp.where(count > float(i), hits[i], hits[0]) for i in range(1, CHUNK)]
            pick = jnp.concatenate(tiles, axis=0).astype(jnp.bfloat16)
            out_ref[b] = jnp.dot(
                pick, vectors[u * bl : (u + 1) * bl], preferred_element_type=jnp.float32
            ).astype(jnp.bfloat16)
            doc = doc_ref[start + b : start + b + 1, :]
            n = jnp.sum((doc == sub).astype(jnp.float32), axis=1, keepdims=True)
            n = jnp.broadcast_to(n, (8, dim)).astype(jnp.int32)
            more = jnp.maximum(chunks(n - 1), 0)
            first = jnp.dot(
                earlier, more.astype(jnp.float32), preferred_element_type=jnp.float32
            ).astype(jnp.int32)
            meta_ref[b, 0] = n
            meta_ref[b, 1] = more
            for j in range(FURTHER):
                meta_ref[b, 2 + j] = jnp.maximum(jnp.minimum(more - 1, j), 0) + jnp.minimum(first, 7)


def vectors_of(h, w):
    projected = jnp.dot(h.reshape(-1, h.shape[-1]), w, preferred_element_type=jnp.float32)
    total = jnp.sum(projected * projected, axis=1, keepdims=True)
    return (projected * lax.rsqrt(total + 1e-06)).astype(jnp.bfloat16)


def pack_first_kernel(
    h_hbm, w_hbm, doc_hbm, live_hbm, out_ref, meta_ref, next_ref, w_ref, row_ref, doc_ref, *scratch
):
    h_ref, token_ref, live_ref, sems = scratch
    nb, count = h_ref.shape[0], next_ref.shape[0]
    groups = nb // GROUP
    small = [
        pltpu.make_async_copy(doc_hbm, token_ref, sems.at[0]),
        pltpu.make_async_copy(live_hbm, live_ref, sems.at[1]),
        pltpu.make_async_copy(w_hbm, w_ref, sems.at[2]),
    ]
    large = [
        pltpu.make_async_copy(
            h_hbm.at[pl.ds(g * GROUP, GROUP)], h_ref.at[pl.ds(g * GROUP, GROUP)], sems.at[4 + g]
        )
        for g in range(groups)
    ]
    later = pltpu.make_async_copy(h_hbm.at[pl.ds(nb, count)], next_ref, sems.at[3])
    for copy in small + large + [later]:
        copy.start()
    small[0].wait()
    small[1].wait()
    row, doc = place_tokens(token_ref[...], live_ref[...] == 1)
    row_ref[...] = row
    doc_ref[...] = doc
    small[2].wait()
    for copy in large:
        copy.wait()

    def project(g):
        return vectors_of(h_ref[g * GROUP : (g + 1) * GROUP], w_ref[...])

    once(lambda: pack_blocks(project, groups, w_ref, row_ref, doc_ref, 0, out_ref, meta_ref))
    later.wait()


def pack_next_kernel(h_ref, w_ref, row_ref, doc_ref, *refs, start, more):
    nb = h_ref.shape[0]
    if more:
        h_hbm, out_ref, meta_ref, next_ref, sem = refs
        later = pltpu.make_async_copy(
            h_hbm.at[pl.ds(start + nb, next_ref.shape[0])], next_ref, sem.at[0]
        )
        later.start()
    else:
        out_ref, meta_ref = refs

    def project(g):
        return vectors_of(h_ref[g * GROUP : (g + 1) * GROUP], w_ref[...])

    groups = nb // GROUP
    once(lambda: pack_blocks(project, groups, w_ref, row_ref, doc_ref, start, out_ref, meta_ref))
    if more:
        later.wait()


def pack(hidden_states, proj_weight, token_doc, token_live):
    nblocks, bl, d = hidden_states.shape
    dim = proj_weight.shape[1]
    sizes = [nblocks * share // sum(PARTS) for share in PARTS]
    starts = [sum(sizes[:i]) for i in range(len(sizes))]
    hidden = in_hbm(hidden_states)

    def outputs(i):
        shapes = [
            pltpu.VMEM((sizes[i], ROWS, dim), jnp.bfloat16),
            pltpu.VMEM((sizes[i], 2 + FURTHER, 8, dim), jnp.int32),
        ]
        if i + 1 < len(sizes):
            shapes.append(pltpu.VMEM((sizes[i + 1], bl, d), hidden_states.dtype))
        return shapes

    def cost(i):
        tokens = sizes[i] * bl
        return pl.CostEstimate(
            flops=2 * tokens * d * dim, bytes_accessed=2 * tokens * d, transcendentals=tokens
        )

    def first():
        shapes = outputs(0) + [
            pltpu.VMEM((d, dim), proj_weight.dtype),
            pltpu.VMEM((nblocks, bl), jnp.int32),
            pltpu.VMEM((nblocks, bl), jnp.int32),
        ]
        return pl.pallas_call(
            pack_first_kernel,
            in_specs=[pl.BlockSpec(memory_space=pltpu.HBM)] * 4,
            out_specs=[VMEM] * len(shapes),
            out_shape=shapes,
            scratch_shapes=[
                pltpu.VMEM((sizes[0], bl, d), hidden_states.dtype),
                pltpu.VMEM((nblocks, bl), jnp.int32),
                pltpu.VMEM((nblocks, bl), jnp.int32),
                pltpu.SemaphoreType.DMA((4 + sizes[0] // GROUP,)),
            ],
            cost_estimate=cost(0),
            compiler_params=PARAMS,
            name="pack_first",
        )(hidden, *(in_hbm(x) for x in (proj_weight, token_doc, token_live)))

    def following(i, fetched, weight, row, doc):
        more = i + 1 < len(sizes)
        return pl.pallas_call(
            functools.partial(pack_next_kernel, start=starts[i], more=more),
            in_specs=[VMEM] * 4 + [pl.BlockSpec(memory_space=pltpu.HBM)] * more,
            out_specs=[VMEM] * (3 if more else 2),
            out_shape=outputs(i),
            scratch_shapes=[pltpu.SemaphoreType.DMA((1,))] * more,
            cost_estimate=cost(i),
            compiler_params=PARAMS,
            name="pack_next",
        )(fetched, weight, row, doc, *[hidden] * more)

    packed, meta = [], []
    for i in range(len(sizes)):
        if i == 0:
            vectors, layout, *left, weight, row, doc = first()
        else:
            vectors, layout, *left = following(i, left[0], weight, row, doc)
        packed.append(vectors)
        meta.append(layout)
    return packed, meta


def score_kernel(owner_ref, *refs, parts, pieces, piece, skipped, width):
    vec_refs, meta_refs = refs[:parts], refs[parts : 2 * parts]
    got_refs = refs[2 * parts : 2 * parts + pieces]
    keep_ref, send_ref, unit_ref, query_ref, table_ref = refs[2 * parts + pieces :]
    n = lax.axis_size("wide")
    bits = n.bit_length() - 1
    me = lax.axis_index("wide")
    columns = query_ref.shape[0]
    quarter = n // 4
    groups = columns // (quarter * piece)
    largest = [jnp.zeros((16, query_ref.shape[1]), jnp.float32) for _ in range(groups)]
    done = 0
    for got_ref in got_refs:
        for k in range(got_ref.shape[0] // piece):
            chip = (me >> 1) ^ bit_reverse(skipped + done, bits - 1)
            group = done // quarter
            place = (chip >> 1) + group * quarter
            block = got_ref[k * piece : (k + 1) * piece, :]
            query_ref[pl.ds(pl.multiple_of(place * piece, piece), piece), :] = block
            size = jnp.abs(block.astype(jnp.float32))
            for r in range(0, piece, 16):
                largest[group] = jnp.maximum(largest[group], size[r : r + 16])
            done += 1
    factors = []
    for group in range(groups):
        unit = jnp.max(jnp.max(largest[group], axis=1, keepdims=True), axis=0, keepdims=True)
        unit = jnp.where(unit > 0.0, unit, 1.0) * (1.0 / SCALE)
        unit_ref[group] = jnp.broadcast_to(unit, unit_ref.shape[1:])
        factors.append(1.0 / unit)
    table_ref[...] = jnp.full(table_ref.shape, LOW, jnp.float32)
    span = min(columns, 512)

    def visit(vec_ref, meta_ref, b, offset, start):
        tokens = vec_ref[pl.ds(b, TOGETHER)].reshape(TOGETHER * ROWS, -1)
        for t in range(span // width):
            at = pl.ds(start + t * width, width)
            similar = lax.dot_general(
                tokens,
                query_ref[at, :],
                (((1,), (1,)), ((), ())),
                preferred_element_type=jnp.float32,
            )
            for u in range(TOGETHER):
                merge(similar[u * ROWS : (u + 1) * ROWS], meta_ref, b + u, offset, at)

    def merge(similar, meta_ref, b, offset, at):
        rows = pl.ds(pl.multiple_of(owner_ref[offset + b] * DOC_DEV, DOC_DEV), DOC_DEV)
        some = [meta_ref[b, tile] > 0 for tile in range(2)]
        index = [meta_ref[b, 2 + j] for j in range(FURTHER)]
        first, rest = (
            functools.reduce(
                jnp.maximum,
                [similar[base + 8 * g : base + 8 * g + 8] for g in range(CHUNK)],
            )
            for base in (0, ROWS // 2)
        )
        best = []
        for c in range(width // 128):
            lanes = slice(c * 128, (c + 1) * 128)
            further = functools.reduce(
                jnp.maximum, [jnp.take_along_axis(rest[:, lanes], at8, axis=0) for at8 in index]
            )
            top = jnp.where(some[0], first[:, lanes], LOW)
            best.append(jnp.maximum(top, jnp.where(some[1], further, LOW)))
        table_ref[rows, at] = jnp.maximum(table_ref[rows, at], jnp.concatenate(best, axis=1))

    def over_blocks(start):
        offset = 0
        for vec_ref, meta_ref in zip(vec_refs, meta_refs):
            nb = vec_ref.shape[0]
            step = next(s for s in (UNROLL, 24, 16, 8) if nb % s == 0)

            def some_blocks(i, carry, vec_ref=vec_ref, meta_ref=meta_ref, offset=offset, step=step):
                for u in range(0, step, TOGETHER):
                    visit(vec_ref, meta_ref, i * step + u, offset, start)
                return carry

            lax.fori_loop(0, nb // step, some_blocks, 0)
            offset += nb

    if columns == span:
        over_blocks(0)
    else:

        def one_span(i, carry):
            over_blocks(pl.multiple_of(i * span, span))
            return carry

        lax.fori_loop(0, columns // span, one_span, 0)
    size = columns // groups
    for place in range(n):
        high = bit_reverse(place % (n // 2), bits - 1)
        high = (high & ~3) | ((high & 1) << 1) | ((high >> 1) & 1)
        owner = me ^ (high << 1 | (place // (n // 2) ^ parity(high, bits)))
        rows = table_ref[pl.ds(pl.multiple_of(owner * DOC_DEV, DOC_DEV), DOC_DEV), :]
        out_ref = send_ref if place >= n // 2 else keep_ref
        start = place % (n // 2) * DOC_DEV
        for group, factor in enumerate(factors):
            at = slice(group * size, (group + 1) * size)
            out_ref[start : start + DOC_DEV, at] = jnp.maximum(rows[:, at] * factor, NONE)


def score(owner, packed, meta, gathered, owners, piece, skipped):
    dim = gathered[0].shape[1]
    columns = sum(piece.shape[0] for piece in gathered)
    rows = sum(p.shape[0] * p.shape[1] for p in packed)
    half = (owners * DOC_DEV // 2, columns)
    return pl.pallas_call(
        functools.partial(
            score_kernel,
            parts=len(packed),
            pieces=len(gathered),
            piece=piece,
            skipped=skipped,
            width=256,
        ),
        in_specs=[pl.BlockSpec(memory_space=pltpu.SMEM)] + [VMEM] * (2 * len(packed) + len(gathered)),
        out_specs=[VMEM] * 3,
        out_shape=[
            pltpu.VMEM(half, jnp.float32),
            pltpu.VMEM(half, jnp.float32),
            pltpu.VMEM((4 * columns // (owners * piece), 8, 128), jnp.float32),
        ],
        scratch_shapes=[
            pltpu.VMEM((columns, dim), jnp.bfloat16),
            pltpu.VMEM((owners * DOC_DEV, columns), jnp.float32),
        ],
        cost_estimate=pl.CostEstimate(
            flops=2 * rows * dim * columns, bytes_accessed=4 * rows * dim, transcendentals=0
        ),
        compiler_params=PARAMS,
    )(owner, *packed, *meta, *(in_vmem(x) for x in gathered))


def in_hbm(x):
    return pltpu.with_memory_space_constraint(x, pltpu.HBM)


def in_vmem(x):
    return pltpu.with_memory_space_constraint(x, pltpu.VMEM)


def finish_kernel(keep_ref, got_ref, unit_1_ref, unit_2_ref, unit_b_ref, out_ref):
    best = jnp.maximum(keep_ref[...], got_ref[...])
    best = jnp.where(best > 0.9 * NONE, best, 0.0)
    size = best.shape[1] // 4
    units = [unit_1_ref[0], unit_2_ref[0], unit_b_ref[0], unit_b_ref[1]]
    quarters = [
        best[:, i * size : (i + 1) * size] * unit[:1, :1] for i, unit in enumerate(units)
    ]
    bits = lax.axis_size("wide").bit_length() - 1
    me = lax.axis_index("wide")
    odd = parity(me, bits) == 1
    turned = (me >> 1) & 1 == 1
    ordered = [quarters[:2], quarters[2:]]
    ordered = [[jnp.where(turned, q[1 - i], q[i]) for i in range(2)] for q in ordered]
    ordered = [[jnp.where(odd, ordered[1 - p][i], ordered[p][i]) for i in range(2)] for p in range(2)]
    low = lax.broadcasted_iota(jnp.int32, (best.shape[0], 128), 1) < 64
    for chip in range(out_ref.shape[1] // 128):
        place = chip // 2
        at = slice(place // 2 * 128, place // 2 * 128 + 128)
        p = parity(chip, bits)
        a, b = ordered[p][chip % 2][:, at], ordered[1 - p][chip % 2][:, at]
        if place % 2:
            a = pltpu.roll(a, 64, 1)
        else:
            b = pltpu.roll(b, 64, 1)
        out_ref[:, chip * 128 : (chip + 1) * 128] = jnp.where(low, a, b)


def finish(*values):
    return pl.pallas_call(
        finish_kernel,
        in_specs=[VMEM] * len(values),
        out_specs=VMEM,
        out_shape=jax.ShapeDtypeStruct(values[0].shape, jnp.float32),
        compiler_params=PARAMS,
        name="finish",
    )(*(in_vmem(x) for x in values))


def program(hidden_states, block_owner, token_doc, token_live, proj_weight, queries):
    n = lax.axis_size("wide")
    if n & (n - 1) or n < 16 or queries.shape[0] != 64:
        raise ValueError("sizes")

    def swap(x, stride):
        return lax.ppermute(x, "wide", [(i, i ^ stride) for i in range(n)])

    strides = [1] + [(1 << bit) | 1 for bit in range(1, n.bit_length() - 1)]
    packed, meta = pack(hidden_states, proj_weight, token_doc, token_live)
    pieces, mine = [queries], queries
    for stride in reversed(strides[1:]):
        pieces.append(swap(mine, stride))
        mine = lax.optimization_barrier(jnp.concatenate([mine, pieces[-1]], axis=0))
    other = swap(mine, 1)
    owner = block_owner.reshape(-1)
    piece = queries.shape[0]
    keep_1, send_1, unit_1 = score(owner, packed, meta, pieces[:-1], n, piece, 0)
    keep_2, send_2, unit_2 = score(owner, packed, meta, pieces[-1:], n, piece, n // 4)
    got_b = swap(jnp.concatenate([send_1, send_2], axis=1).astype(SENT), 1)
    keep_b, send_b, unit_b = score(owner, packed, meta, [other], n, piece, 0)
    got_a = swap(send_b.astype(SENT), 1)
    best = jnp.concatenate(
        [
            jnp.maximum(jnp.concatenate([keep_1, keep_2], axis=1), got_a.astype(jnp.float32)),
            jnp.maximum(keep_b, got_b.astype(jnp.float32)),
        ],
        axis=1,
    )
    quarter = best.shape[1] // 4
    for stride in [strides[2], strides[1]] + strides[3:]:
        half = best.shape[0] // 2
        keep, got = best[:half], swap(best[half:].astype(SENT), stride)
        if stride == strides[1]:
            got = jnp.concatenate([got[:, i * quarter : (i + 1) * quarter] for i in (1, 0, 3, 2)], axis=1)
        if stride != strides[-1]:
            best = jnp.maximum(keep, got.astype(jnp.float32))
    return finish(keep, got.astype(jnp.float32), unit_1, unit_2, unit_b)


def solution(mesh):
    placed = (
        P(("groups", "wide"), None, None),
        P(("groups", "wide"), None),
        P(("groups", "wide"), None),
        P(("groups", "wide"), None),
        P(),
        P(("groups", "wide"), None),
    )
    return jax.shard_map(
        program, mesh=mesh, in_specs=placed, out_specs=P(("groups", "wide"), None), check_vma=False
    )
```
